768 devices in a mesh: ctx: 64 (over x, y, core), exp: 12 (over z).
Axes of the slice: x: 4, y: 8, z: 12, core: 2. Of those that a mesh axis runs over, the one named last changes fastest.
Arguments:
- queries: bfloat16 [8192, 6144], P('ctx', 'exp'), may hold values from -0.71875 to 0.71875
- keys: bfloat16 [8192, 6144], P('ctx', 'exp'), may hold values from -0.71875 to 0.71875
- values: bfloat16 [8192, 6144], P('ctx', 'exp'), may hold values from -0.71875 to 0.71875
- out_grad: bfloat16 [8192, 6144], P('ctx', 'exp'), may hold values from -0.71875 to 0.71875
- log_decay: float32 [8192, 48], P('ctx', 'exp'), may hold values from -1.6 to 0, as said below
- moe_grad: bfloat16 [8192, 6144], P('ctx', 'exp'), may hold values from -6 to 6
- expert_ids: int32 [8192, 2], P('ctx'), may hold values from 0 to 31, all different within a row; in each aligned block of 128 rows (0 to 127, 128 to 255, ...) at most 10 rows name the same one
- gate_weights: float32 [8192, 2], P('ctx'), may hold values from 0.2 to 1
- down_weight: bfloat16 [64, 3072, 6144], P('ctx', 'exp'), may hold values from -0.078125 to 0.078125
Outputs:
- query_grad: bfloat16 [8192, 6144], P('ctx', 'exp')
- key_grad: bfloat16 [8192, 6144], P('ctx', 'exp')
- value_grad: bfloat16 [8192, 6144], P('ctx', 'exp')
- hidden_grad: bfloat16 [64, 640, 3072], P('ctx', None, 'exp')
The draws below stay inside these ranges and needn't reach their ends.
Inputs may be any that keep to these rules, and one draw needn't show every extreme that they name: `expert_ids`: in the rows of one device (aligned blocks of 128 tokens) no expert is named more than 10 times, and in every draw some expert is named exactly 10 times in some block; a token's two experts differ. `log_decay`: every entry is negative.
All inputs are finite; a program needn't handle non-finite values.
Results may differ from the reference program's by a relative error of at most 0.0049.
Values may be sent and summed in bfloat16 or wider, within the bound.
No kernel may reach another device: no remote copies, remote signals or barrier semaphores. Data moves between devices by JAX's collectives and lax.ppermute only.
A program may use at most 128 MiB of HBM per device.

```python
import math
import jax
import jax.numpy as jnp
import numpy as np
from jax import lax

D = 6144
FF = 6144
HEAD_TOTAL = 48
HD = 128
TOK_DEV = 128
EXPERTS = 32
CAP = 10
TOKEN_TOTAL = 8192


def draw_log_decay(key, part):
    folded = jax.random.fold_in(key, 7)
    pick_key, slow_key, fast_key, rough_key, location_random_key, loss_random_key = jax.random.split(folded, 6)
    fast_share = 0.5
    is_fast = jax.random.uniform(pick_key, (HEAD_TOTAL,)) < fast_share
    slow_rate = jnp.exp(jax.random.uniform(slow_key, (HEAD_TOTAL,), minval=jnp.log(0.2), maxval=jnp.log(0.8))) / TOKEN_TOTAL
    fast_rate = jnp.exp(jax.random.uniform(fast_key, (HEAD_TOTAL,), minval=jnp.log(1.0 / 50.0), maxval=jnp.log(1.0 / 30.0)))
    decay_factor = jnp.where(is_fast, fast_rate, slow_rate)
    jaggedness = jax.random.uniform(rough_key, (TOKEN_TOTAL, HEAD_TOTAL), minval=0.5, maxval=1.5)
    spike_locations = jax.random.randint(location_random_key, (2, HEAD_TOTAL), 0, TOKEN_TOTAL)
    spike_loss = jnp.log(jax.random.uniform(loss_random_key, (2, HEAD_TOTAL), minval=0.5, maxval=0.8))
    position_indices = jnp.arange(TOKEN_TOTAL)[:, None, None] == spike_locations[None]
    spike_total_sum = jnp.sum(jnp.where(position_indices, spike_loss[None], 0.0), axis=1)
    return (-decay_factor[None, :] * jaggedness + spike_total_sum).astype(jnp.float32)


def steps_of(rng, extent, shards, low, top_value):
    factor_of = 1.0
    for position, parts in shards:
        steps = jax.random.uniform(jax.random.fold_in(jax.random.fold_in(rng, 6), position), (parts,), jnp.float32, low / len(shards), top_value / len(shards))
        factor_of = factor_of * jnp.repeat(jnp.exp(steps), extent[position] // parts).reshape((-1,) + (1,) * (len(extent) - 1 - position))
    return factor_of


def deal_out(own_key, own, number, rows, amount, top, limit, slope):
    ranking = jax.random.permutation(own_key, amount)
    heavy_load, common = shares(amount, rows * top, limit, slope, True), shares(amount, rows * top, limit, slope, False)
    places = jnp.arange(amount)

    def named(tallies, offset_by):
        used = int((tallies > 0).sum())
        fixed = max(1, used // 4)
        moved = fixed + (places - fixed + offset_by * (used - fixed)) % max(1, amount - fixed)
        return jnp.zeros((amount,), jnp.int32).at[ranking[jnp.where(places < fixed, places, moved)]].set(jnp.asarray(tallies, jnp.int32))

    tallies = jnp.where(number % 4 == 0, named(heavy_load, number // 4), named(common, number - number // 4 - 1))
    mixed = jax.random.permutation(jax.random.fold_in(own, 3), amount)
    giver, sink = mixed[0:amount // 2 * 2:2], mixed[1:amount // 2 * 2:2]
    margin = jnp.minimum(tallies[giver] - 1, limit - tallies[sink]) // 2
    margin = jnp.where((giver == ranking[0]) | (sink == ranking[0]) | (tallies[sink] == 0), 0, jnp.maximum(margin, 0))
    moved = jax.random.randint(jax.random.fold_in(own, 4), (amount // 2,), 0, 1 << 20) % (margin + 1)
    tallies = tallies.at[giver].add(-moved).at[sink].add(moved)
    labels = jnp.searchsorted(jnp.cumsum(tallies), jnp.arange(rows * top), side="right").astype(jnp.int32)
    listing = labels.reshape(top, rows).T
    listing = listing[jax.random.permutation(jax.random.fold_in(own, 1), rows)]
    offset_by = jax.random.randint(jax.random.fold_in(own, 2), (rows, 1), 0, top)
    return jnp.take_along_axis(listing, (jnp.arange(top)[None, :] + offset_by) % top, axis=1)


def shares(amount, total, bound, slope, full):
    weights = [(1 << 20) // math.isqrt(rank ** slope) + 1 for rank in range(1, amount + 1)]
    largest = bound if full else min(bound, max(-(-total // amount), total * weights[0] // sum(weights)))
    least = 1 if total - largest >= amount - 1 else 0
    given, surplus = [largest] + [least] * (amount - 1), total - largest - least * (amount - 1)
    while surplus > 0:
        candidates = [i for i in range(1, amount) if given[i] < largest] or [i for i in range(1, amount) if given[i] < bound]
        pool, budget = sum([weights[i] for i in candidates]), surplus
        for i in candidates:
            more = min(bound - given[i], max(1, budget * weights[i] // pool), surplus)
            given[i] = given[i] + more
            surplus = surplus - more
    return np.array(given)


def noise(rng, shape, deviation, bound, cuts=(), dtype=jnp.bfloat16):
    loudness = steps_of(rng, shape, cuts, -0.22, 0.18) if cuts else 1.0
    entries = jax.random.normal(rng, shape, jnp.float32) * deviation * loudness
    return jnp.minimum(jnp.maximum(entries, -bound), bound).astype(dtype)


def setup_inputs(seed: int = 0) -> dict:
    splits = jax.random.split(jax.random.key(seed), 10)
    queries = noise(splits[0], (TOKEN_TOTAL, HEAD_TOTAL * HD), 0.12, 0.71875, ((0, 64), (1, 12)))
    keys = noise(splits[1], (TOKEN_TOTAL, HEAD_TOTAL * HD), 0.12, 0.71875, ((0, 64), (1, 12)))
    values = noise(splits[2], (TOKEN_TOTAL, HEAD_TOTAL * HD), 0.12, 0.71875, ((0, 64), (1, 12)))
    out_grad = noise(splits[3], (TOKEN_TOTAL, HEAD_TOTAL * HD), 0.12, 0.71875, ((0, 64), (1, 12)))
    log_decay = draw_log_decay(jax.random.fold_in(splits[9], 71), 0)
    moe_grad = noise(splits[5], (TOKEN_TOTAL, D), 1.0, 6.0, ((0, 64), (1, 12)))
    expert_ids_keys = jax.random.split(jax.random.fold_in(splits[6], 1), TOKEN_TOTAL // TOK_DEV)
    expert_ids_turns = jax.random.permutation(jax.random.fold_in(splits[6], 3), TOKEN_TOTAL // TOK_DEV)
    expert_ids = jax.vmap(lambda own, number: deal_out(jax.random.fold_in(splits[6], 2), own, number, TOK_DEV, EXPERTS, 2, CAP, 1))(expert_ids_keys, expert_ids_turns).reshape((TOKEN_TOTAL, 2))
    gate_weights = jnp.clip(0.2 + 0.8 * jax.random.uniform(splits[7], (TOKEN_TOTAL, 2), jnp.float32) ** steps_of(splits[7], (TOKEN_TOTAL, 2), ((0, 64),), -0.2, 0.2), 0.2, 1.0)
    down_weight = noise(splits[8], (2 * EXPERTS, FF // 2, D), FF ** -0.5, 0.078125, ((0, 64), (1, 12)))
    return dict(queries=queries, keys=keys, values=values, out_grad=out_grad, log_decay=log_decay, moe_grad=moe_grad, expert_ids=expert_ids, gate_weights=gate_weights, down_weight=down_weight)


def head_grads(inputs):
    query_h, key_h, value_h, grad_h, decay_h = inputs
    running = jnp.cumsum(decay_h, axis=1)
    closing = running[:, -1]
    length = running.shape[1]
    causal = jnp.arange(length)[:, None] >= jnp.arange(length)[None, :]
    spread = running[:, :, None] - running[:, None, :]
    weights = jnp.where(causal[None], jnp.exp(jnp.where(causal[None], spread, 0.0)), 0.0)
    query_full = query_h.astype(jnp.float32)
    key_full = key_h.astype(jnp.float32)
    value_full = value_h.astype(jnp.float32)
    gradient_full = grad_h.astype(jnp.float32)
    until_finish = jnp.exp(closing[:, None] - running)
    since_beginning = jnp.exp(running)
    block_state = jnp.einsum("bsk,bsv->bkv", key_full * until_finish[:, :, None], value_full, precision=lax.Precision.HIGHEST)
    block_grad = jnp.einsum("btk,btv->bkv", query_full * since_beginning[:, :, None], gradient_full, precision=lax.Precision.HIGHEST)
    block_decay = jnp.exp(closing)

    def forward_step(carried, block_item):
        state_in, decay_in = block_item
        return decay_in * carried + state_in, carried

    zero_state = jnp.zeros(block_state.shape[1:], jnp.float32)
    _, leading_part = lax.scan(forward_step, zero_state, (block_state, block_decay))
    _, trailing_part = lax.scan(forward_step, zero_state, (block_grad, block_decay), reverse=True)
    grad_scores = (jnp.einsum("btv,bsv->bts", gradient_full, value_full) * weights).astype(jnp.bfloat16)
    grad_scores = lax.optimization_barrier(grad_scores).astype(jnp.float32)
    scores = (jnp.einsum("btk,bsk->bts", query_full, key_full) * weights).astype(jnp.bfloat16)
    scores = lax.optimization_barrier(scores).astype(jnp.float32)
    query_grad = jnp.einsum("bts,bsk->btk", grad_scores, key_full) + since_beginning[:, :, None] * jnp.einsum("btv,bkv->btk", gradient_full, leading_part, precision=lax.Precision.HIGHEST)
    key_grad = jnp.einsum("bts,btk->bsk", grad_scores, query_full) + until_finish[:, :, None] * jnp.einsum("bsv,bkv->bsk", value_full, trailing_part, precision=lax.Precision.HIGHEST)
    value_grad = jnp.einsum("bts,btv->bsv", scores, gradient_full) + until_finish[:, :, None] * jnp.einsum("bsk,bkv->bsv", key_full, trailing_part, precision=lax.Precision.HIGHEST)
    return (query_grad.astype(jnp.bfloat16), key_grad.astype(jnp.bfloat16), value_grad.astype(jnp.bfloat16))


def reference(queries, keys, values, out_grad, log_decay, moe_grad, expert_ids, gate_weights, down_weight):
    blocks = TOKEN_TOTAL // TOK_DEV

    def per_head(stacked):
        return stacked.reshape(blocks, TOK_DEV, HEAD_TOTAL, HD).transpose(2, 0, 1, 3)

    def merge_heads(stacked):
        return stacked.transpose(1, 2, 0, 3).reshape(TOKEN_TOTAL, HEAD_TOTAL * HD)

    decay_heads = log_decay.reshape(blocks, TOK_DEV, HEAD_TOTAL).transpose(2, 0, 1)
    outputs = lax.map(head_grads, (per_head(queries), per_head(keys), per_head(values), per_head(out_grad), decay_heads))
    query_grad = merge_heads(outputs[0])
    key_grad = merge_heads(outputs[1])
    value_grad = merge_heads(outputs[2])

    pair_ids = expert_ids.reshape(blocks, 2 * TOK_DEV)
    pair_gates = gate_weights.reshape(blocks, 2 * TOK_DEV)
    onehot = (pair_ids[:, :, None] == jnp.arange(EXPERTS)[None, None, :]).astype(jnp.int32)
    earlier = jnp.cumsum(onehot, axis=1) - onehot
    pair_ranks = jnp.sum(earlier * onehot, axis=2)
    pair_slots = pair_ids * CAP + pair_ranks
    grad_blocks = moe_grad.reshape(blocks, TOK_DEV, D)

    def route_block(inputs):
        slot_row, gate_row, grad_rows = inputs
        dispatch_table = (jnp.arange(EXPERTS * CAP)[:, None] == slot_row[None, :]).astype(jnp.float32) * gate_row[None, :]
        dispatch_table = dispatch_table.reshape(EXPERTS * CAP, TOK_DEV, 2).sum(axis=2)
        return jnp.dot(dispatch_table, grad_rows.astype(jnp.float32), precision=lax.Precision.HIGHEST).astype(jnp.bfloat16)

    routed = lax.map(route_block, (pair_slots, pair_gates, grad_blocks))
    routed = routed.reshape(blocks, EXPERTS, CAP, D).transpose(1, 0, 2, 3).reshape(EXPERTS, blocks * CAP, D)
    halves = down_weight.reshape(EXPERTS, FF, D)

    def expert_block(inputs):
        expert_rows, expert_weight = inputs
        product = jnp.dot(expert_rows, expert_weight.T, preferred_element_type=jnp.float32).astype(jnp.bfloat16)
        return product.reshape(blocks * CAP, 2, FF // 2).transpose(1, 0, 2)

    hidden_grad = lax.map(expert_block, (routed, halves)).reshape(2 * EXPERTS, blocks * CAP, FF // 2)
    return (query_grad, key_grad, value_grad, hidden_grad)
```

```python
import functools

import jax
import jax.numpy as jnp
from jax import lax
from jax.experimental import pallas as pl
from jax.experimental.pallas import tpu as pltpu
from jax.sharding import Mesh, PartitionSpec as P

F32 = jnp.float32
BF16 = jnp.bfloat16
LANES = 128
HEAD = 128
WHOLE = 8
INTERPRET = False


def call(kernel, out_shape, flops, moved, **options):
    return pl.pallas_call(
        kernel,
        out_shape=out_shape,
        interpret=INTERPRET,
        cost_estimate=pl.CostEstimate(flops=flops, bytes_accessed=moved, transcendentals=0),
        **options,
    )


def matmul(a, b):
    return lax.dot_general(a, b, (((1,), (0,)), ((), ())), preferred_element_type=F32)


def matmul_t(a, b):
    return lax.dot_general(a, b, (((1,), (1,)), ((), ())), preferred_element_type=F32)


def pieces(x):
    high = x.astype(BF16)
    rest = x - high.astype(F32)
    middle = rest.astype(BF16)
    return high, middle, (rest - middle.astype(F32)).astype(BF16)


def square(n):
    return (
        lax.broadcasted_iota(jnp.int32, (n, n), 0),
        lax.broadcasted_iota(jnp.int32, (n, n), 1),
    )


def as_row(column, eye):
    return jnp.sum(jnp.where(eye, column, 0.0), axis=0, keepdims=True)


def running_sums(log_decay, row, col):
    lower = jnp.where(row >= col, 1.0, 0.0).astype(BF16)
    high, middle, low = pieces(log_decay)
    return matmul(lower, high) + (matmul(lower, middle) + matmul(lower, low))


def route_kernel(experts, capacity, ids_ref, gate_ref, grad_ref, out_ref):
    length, width = grad_ref.shape
    groups = width // LANES
    tail = capacity - WHOLE
    rows = groups * capacity
    row, col = square(length)
    eye = row == col
    ids = ids_ref[...].astype(F32)
    grad = grad_ref[...].astype(F32)
    names = [as_row(ids[:, j : j + 1], eye) for j in range(2)]
    numbers = lax.broadcasted_iota(jnp.int32, (experts, length), 0).astype(F32)
    chosen = [jnp.where(numbers == name, 1.0, 0.0) for name in names]
    before = jnp.where(row < col, 1.0, 0.0).astype(BF16)
    counts = matmul((chosen[0] + chosen[1]).astype(BF16), before)
    ranks = [jnp.sum(one * counts, axis=0, keepdims=True) for one in chosen]
    scaled = [(gate_ref[:, j : j + 1] * grad).astype(BF16) for j in range(2)]
    chunk = 8
    while experts % chunk:
        chunk //= 2
    for start in range(0, experts, chunk):
        place = lax.broadcasted_iota(jnp.int32, (chunk * rows, 2 * length), 0) + start * rows
        total = None
        for f in range(groups):
            codes = [
                name * rows
                + jnp.where(
                    rank < WHOLE, rank + f * WHOLE, rank + (groups * WHOLE + f * tail - WHOLE)
                )
                for name, rank in zip(names, ranks)
            ]
            code = jnp.concatenate(codes, axis=1).astype(jnp.int32)
            table = jnp.where(place == code, 1.0, 0.0).astype(BF16)
            part = jnp.concatenate([one[:, f * LANES : (f + 1) * LANES] for one in scaled], axis=0)
            product = matmul(table, part)
            total = product if total is None else total + product
        out_ref[start : start + chunk] = total.reshape(chunk, rows, LANES).astype(BF16)


def state_kernel(share, query_ref, key_ref, value_ref, grad_ref, decay_ref, out_ref):
    length, heads = decay_ref.shape
    row, col = square(length)
    eye = row == col
    running = running_sums(decay_ref[...], row, col)
    per_head = HEAD // share
    lines = lax.broadcasted_iota(jnp.int32, (share, LANES), 0)
    for h in range(heads):
        lanes = slice(h * HEAD, (h + 1) * HEAD)
        since = as_row(running[:, h : h + 1], eye)
        closing = running[length - 1 : length, h : h + 1]
        places = slice(h * per_head, (h + 1) * per_head)
        for at, left, right, factor in (
            (0, key_ref, value_ref, jnp.exp(closing - since)),
            (share, query_ref, grad_ref, jnp.exp(since)),
        ):
            turned = left[:, lanes].astype(F32).T * factor
            high = turned.astype(BF16)
            low = (turned - high.astype(F32)).astype(BF16)
            state = matmul(high, right[:, lanes]) + matmul(low, right[:, lanes])
            out_ref[places, at : at + share] = state.astype(BF16).reshape(per_head, share, LANES)
        high, middle, low = [
            part.astype(F32) for part in pieces(jnp.broadcast_to(jnp.exp(closing), (share, LANES)))
        ]
        decay = jnp.where(lines == 0, high, jnp.where(lines == 1, middle, low))
        out_ref[places, 2 * share : 3 * share] = jnp.broadcast_to(
            decay[None], (per_head, share, LANES)
        ).astype(BF16)


def scan_kernel(share, in_ref, out_ref):
    blocks = in_ref.shape[0]

    def step(carried, b, at):
        held = in_ref[b].astype(F32)
        decay = (held[2 * share : 2 * share + 1] + held[2 * share + 1 : 2 * share + 2]) + held[
            2 * share + 2 : 2 * share + 3
        ]
        return carried, decay * carried + held[at : at + share]

    ahead = jnp.zeros((share, LANES), F32)
    behind = jnp.zeros((share, LANES), F32)
    for b in range(blocks):
        now, ahead = step(ahead, b, 0)
        out_ref[b, 0:share] = now
        now, behind = step(behind, blocks - 1 - b, share)
        out_ref[blocks - 1 - b, share : 2 * share] = now


def output_kernel(
    share, query_ref, key_ref, value_ref, grad_ref, decay_ref, carried_ref, dq_ref, dk_ref, dv_ref
):
    length, heads = decay_ref.shape
    row, col = square(length)
    eye = row == col
    running = running_sums(decay_ref[...], row, col)
    per_head = HEAD // share
    for h in range(heads):
        lanes = slice(h * HEAD, (h + 1) * HEAD)
        since = running[:, h : h + 1]
        since_row = as_row(since, eye)
        closing = running[length - 1 : length, h : h + 1]
        carried = carried_ref[h * per_head : (h + 1) * per_head]
        leading = pieces(carried[:, 0:share].reshape(HEAD, LANES))
        trailing = pieces(carried[:, share : 2 * share].reshape(HEAD, LANES))
        q, k, v, g = (ref[:, lanes] for ref in (query_ref, key_ref, value_ref, grad_ref))
        weights = jnp.where(row >= col, jnp.exp(jnp.where(row >= col, since - since_row, 0.0)), 0.0)
        turned = jnp.where(row <= col, jnp.exp(jnp.where(row <= col, since_row - since, 0.0)), 0.0)
        until = jnp.exp(closing - since)
        grad_scores = (matmul_t(g, v) * weights).astype(BF16)
        grad_scores_t = (matmul_t(v, g) * turned).astype(BF16)
        scores_t = (matmul_t(k, q) * turned).astype(BF16)
        dq_ref[:, lanes] = (
            matmul(grad_scores, k) + jnp.exp(since) * (matmul_t(g, leading[0]) + matmul_t(g, leading[1]))
        ).astype(BF16)
        dk_ref[:, lanes] = (
            matmul(grad_scores_t, q)
            + until * (matmul_t(v, trailing[0]) + matmul_t(v, trailing[1]))
        ).astype(BF16)
        dv_ref[:, lanes] = (
            matmul(scores_t, g) + until * (matmul(k, trailing[0]) + matmul(k, trailing[1]))
        ).astype(BF16)


def expert_kernel(capacity, rows_ref, weight_ref, out_ref, total, order):
    step = pl.program_id(0)
    cores, _, sources, lines, _ = rows_ref.shape
    groups = lines // capacity
    tail = capacity - WHOLE
    small = sources * groups * tail
    half = sources * capacity

    @pl.when(step == 0)
    def _():
        row, col = square(small)
        want = (row // tail % sources) * (groups * tail) + (row // (tail * sources)) * tail + row % tail
        order[...] = jnp.where(col == want, 1.0, 0.0).astype(BF16)
        total[...] = jnp.zeros_like(total)

    held = [rows_ref[c, 0] for c in range(cores)]
    rest = [one[:, groups * WHOLE :].reshape(small, LANES) for one in held]
    rest = matmul(order[...], jnp.concatenate(rest, axis=1)).astype(BF16)
    each = small // groups
    left = []
    for c in range(cores):
        whole = [
            held[c][:, f * WHOLE : (f + 1) * WHOLE].reshape(sources * WHOLE, LANES)
            for f in range(groups)
        ]
        left.append(jnp.concatenate(whole, axis=1))
        ends = rest[:, c * LANES : (c + 1) * LANES]
        left.append(jnp.concatenate([ends[f * each : (f + 1) * each] for f in range(groups)], axis=1))
    total[...] += matmul_t(jnp.concatenate(left, axis=0), weight_ref[...])

    @pl.when(step == pl.num_programs(0) - 1)
    def _():
        row, col = square(cores * half)
        block = row // capacity
        slot = row - block * capacity
        source = block // cores
        line = jnp.where(
            slot < WHOLE, source * WHOLE + slot, sources * WHOLE + source * tail + slot - WHOLE
        )
        want = line + (block - source * cores) * half
        place = jnp.where(col == want, 1.0, 0.0).astype(BF16)
        out_ref[0] = matmul(place, total[...].astype(BF16)).astype(BF16)


def per_device(
    queries, keys, values, out_grad, log_decay, moe_grad, expert_ids, gate_weights, down_weight
):
    chips = lax.axis_size("chip")
    blocks = 2 * chips
    experts = chips
    length, width = moe_grad.shape
    capacity = 5 * length // (2 * experts)
    heads = log_decay.shape[1]
    lines = width // LANES * capacity
    share = heads * HEAD // blocks
    weight = down_weight[0]
    hidden = weight.shape[0]

    sent = call(
        functools.partial(route_kernel, experts, capacity),
        jax.ShapeDtypeStruct((experts, lines, LANES), BF16),
        2 * experts * lines * 2 * length * width,
        experts * lines * LANES * 2 + length * width * 2,
        name="route",
    )(expert_ids, gate_weights, moe_grad)
    arrived = lax.all_to_all(sent, "chip", 0, 0, tiled=True)
    gathered = lax.all_gather(arrived, ("core", "exp"), axis=0)

    states = call(
        functools.partial(state_kernel, share),
        jax.ShapeDtypeStruct((blocks, 3 * share, LANES), BF16),
        8 * heads * length * HEAD * HEAD,
        8 * length * width,
        name="states",
    )(queries, keys, values, out_grad, log_decay)
    states, arrived = lax.optimization_barrier((states, arrived))
    spread = lax.all_to_all(states, ("chip", "core"), 0, 0, tiled=True)
    carried = call(
        functools.partial(scan_kernel, share),
        jax.ShapeDtypeStruct((blocks, 2 * share, LANES), F32),
        8 * blocks * share * LANES,
        10 * blocks * share * LANES,
        name="scan",
    )(spread)
    carried = lax.all_to_all(carried, ("chip", "core"), 0, 0, tiled=True)
    flat = jax.ShapeDtypeStruct((length, width), BF16)
    query_grad, key_grad, value_grad = call(
        functools.partial(output_kernel, share),
        (flat, flat, flat),
        18 * heads * length * HEAD * HEAD,
        14 * length * width,
        name="outputs",
    )(queries, keys, values, out_grad, log_decay, carried)

    places = lax.axis_size("exp")
    rows = 2 * chips * capacity
    hidden_grad = call(
        functools.partial(expert_kernel, capacity),
        jax.ShapeDtypeStruct((1, rows, hidden), BF16),
        2 * rows * width * places * hidden,
        2 * (rows + hidden) * width * places,
        grid=(places,),
        in_specs=[
            pl.BlockSpec((2, 1, chips, lines, LANES), lambda z: (0, z, 0, 0, 0)),
            pl.BlockSpec((hidden, width), lambda z: (0, z)),
        ],
        out_specs=pl.BlockSpec((1, rows, hidden), lambda z: (0, 0, 0)),
        scratch_shapes=[
            pltpu.VMEM((rows, hidden), F32),
            pltpu.VMEM(((capacity - WHOLE) * chips * (width // LANES),) * 2, BF16),
        ],
        name="experts",
    )(gathered.reshape(2, places, chips, lines, LANES), weight)
    return (query_grad, key_grad, value_grad, hidden_grad)


def solution(mesh):
    ctx, exp = mesh.devices.shape
    mesh = Mesh(mesh.devices.reshape(ctx // 2, 2, exp), ("chip", "core", "exp"))
    ctx = ("chip", "core")
    in_specs = (
        P(ctx, "exp"),
        P(ctx, "exp"),
        P(ctx, "exp"),
        P(ctx, "exp"),
        P(ctx, "exp"),
        P(ctx, "exp"),
        P(ctx, None),
        P(ctx, None),
        P(ctx, "exp", None),
    )
    out_specs = (P(ctx, "exp"), P(ctx, "exp"), P(ctx, "exp"), P(ctx, None, "exp"))
    return jax.shard_map(
        per_device, mesh=mesh, in_specs=in_specs, out_specs=out_specs, check_vma=False
    )
```

```python
import functools

import jax
import jax.numpy as jnp
from jax import lax
from jax.experimental import pallas as pl
from jax.experimental.pallas import tpu as pltpu
from jax.sharding import Mesh, PartitionSpec as P

F32 = jnp.float32
BF16 = jnp.bfloat16
LANES = 128
HEAD = 128
WHOLE = 8
TOGETHER = 4
INTERPRET = False


def call(kernel, out_shape, flops, moved, **options):
    return pl.pallas_call(
        kernel,
        out_shape=out_shape,
        interpret=INTERPRET,
        cost_estimate=pl.CostEstimate(flops=flops, bytes_accessed=moved, transcendentals=0),
        **options,
    )


def matmul(a, b):
    return lax.dot_general(a, b, (((1,), (0,)), ((), ())), preferred_element_type=F32)


def matmul_t(a, b):
    return lax.dot_general(a, b, (((1,), (1,)), ((), ())), preferred_element_type=F32)


def pieces(x):
    high = x.astype(BF16)
    rest = x - high.astype(F32)
    middle = rest.astype(BF16)
    return high, middle, (rest - middle.astype(F32)).astype(BF16)


def square(n):
    return (
        lax.broadcasted_iota(jnp.int32, (n, n), 0),
        lax.broadcasted_iota(jnp.int32, (n, n), 1),
    )


def as_column(line, eye):
    return jnp.sum(jnp.where(eye, line, 0.0), axis=1, keepdims=True)


def running_sums(log_decay, row, col):
    upper = jnp.where(row <= col, 1.0, 0.0).astype(BF16)
    high, middle, low = pieces(log_decay)
    return matmul(high, upper) + (matmul(middle, upper) + matmul(low, upper))


def one_hot(want, columns):
    places = lax.broadcasted_iota(jnp.int32, (want.shape[0], columns), 1)
    return jnp.where(places == want, 1.0, 0.0).astype(BF16)


def counting(n):
    return lax.broadcasted_iota(jnp.int32, (n, 1), 0)


def route_kernel(experts, capacity, ids_ref, gate_ref, grad_ref, out_ref):
    length, width = grad_ref.shape
    groups = width // LANES
    tail = capacity - WHOLE
    most = experts * WHOLE
    row, col = square(length)
    eye = row == col
    ids = ids_ref[...].astype(F32)
    grad = grad_ref[...].astype(F32)
    names = [ids[j : j + 1] for j in range(2)]
    numbers = lax.broadcasted_iota(jnp.int32, (experts, length), 0).astype(F32)
    chosen = [jnp.where(numbers == name, 1.0, 0.0) for name in names]
    before = jnp.where(row < col, 1.0, 0.0).astype(BF16)
    counts = matmul((chosen[0] + chosen[1]).astype(BF16), before)
    ranks = [jnp.sum(one * counts, axis=0, keepdims=True) for one in chosen]
    scaled = [(as_column(gate_ref[j : j + 1], eye) * grad).astype(BF16) for j in range(2)]
    codes = [
        jnp.where(rank < WHOLE, name * WHOLE + rank, name * tail + rank + (most - WHOLE))
        for name, rank in zip(names, ranks)
    ]
    code = jnp.concatenate(codes, axis=1).astype(jnp.int32)
    place = lax.broadcasted_iota(jnp.int32, (experts * capacity, 2 * length), 0)
    table = jnp.where(place == code, 1.0, 0.0).astype(BF16)
    routed = matmul(table, jnp.concatenate(scaled, axis=0)).astype(BF16)
    parts = [routed[:, f * LANES : (f + 1) * LANES] for f in range(groups)]
    for f in range(groups):
        out_ref[:, f * WHOLE : (f + 1) * WHOLE] = parts[f][:most].reshape(experts, WHOLE, LANES)
    rest = jnp.concatenate([part[most:] for part in parts], axis=0)
    line = counting(experts * groups * tail)
    expert = line // (groups * tail)
    f = (line - expert * (groups * tail)) // tail
    want = f * (experts * tail) + expert * tail + (line - expert * (groups * tail) - f * tail)
    rest = matmul(one_hot(want, experts * groups * tail), rest).astype(BF16)
    out_ref[:, groups * WHOLE :] = rest.reshape(experts, groups * tail, LANES)


def state_kernel(share, query_ref, key_ref, value_ref, grad_ref, decay_ref, out_ref):
    heads, length = decay_ref.shape
    row, col = square(length)
    running = running_sums(decay_ref[...], row, col)
    per_head = HEAD // share
    lines = lax.broadcasted_iota(jnp.int32, (share, LANES), 0)
    for h in range(heads):
        lanes = slice(h * HEAD, (h + 1) * HEAD)
        since = running[h : h + 1]
        closing = running[h : h + 1, length - 1 : length]
        places = slice(h * per_head, (h + 1) * per_head)
        for at, left, right, factor in (
            (0, key_ref, value_ref, jnp.exp(closing - since)),
            (share, query_ref, grad_ref, jnp.exp(since)),
        ):
            turned = left[:, lanes].astype(F32).T * factor
            high = turned.astype(BF16)
            low = (turned - high.astype(F32)).astype(BF16)
            state = matmul(high, right[:, lanes]) + matmul(low, right[:, lanes])
            out_ref[places, at : at + share] = state.astype(BF16).reshape(per_head, share, LANES)
        high, middle, low = [
            part.astype(F32) for part in pieces(jnp.broadcast_to(jnp.exp(closing), (share, LANES)))
        ]
        decay = jnp.where(lines == 0, high, jnp.where(lines == 1, middle, low))
        out_ref[places, 2 * share : 3 * share] = jnp.broadcast_to(
            decay[None], (per_head, share, LANES)
        ).astype(BF16)


def scan_kernel(share, in_ref, out_ref):
    blocks = in_ref.shape[0]

    def step(carried, b, at):
        held = in_ref[b].astype(F32)
        decay = (held[2 * share : 2 * share + 1] + held[2 * share + 1 : 2 * share + 2]) + held[
            2 * share + 2 : 2 * share + 3
        ]
        return carried, decay * carried + held[at : at + share]

    ahead = jnp.zeros((share, LANES), F32)
    behind = jnp.zeros((share, LANES), F32)
    for b in range(blocks):
        now, ahead = step(ahead, b, 0)
        out_ref[b, 0:share] = now.astype(BF16)
        now, behind = step(behind, blocks - 1 - b, share)
        out_ref[blocks - 1 - b, share : 2 * share] = now.astype(BF16)


def output_kernel(
    share, query_ref, key_ref, value_ref, grad_ref, decay_ref, carried_ref, dq_ref, dk_ref, dv_ref
):
    heads, length = decay_ref.shape
    row, col = square(length)
    eye = row == col
    running = running_sums(decay_ref[...], row, col)
    per_head = HEAD // share
    for h in range(heads):
        lanes = slice(h * HEAD, (h + 1) * HEAD)
        since_row = running[h : h + 1]
        since = as_column(since_row, eye)
        closing = since_row[:, length - 1 : length]
        carried = carried_ref[h * per_head : (h + 1) * per_head]
        leading = carried[:, 0:share].reshape(HEAD, LANES)
        trailing = carried[:, share : 2 * share].reshape(HEAD, LANES)
        q, k, v, g = (ref[:, lanes] for ref in (query_ref, key_ref, value_ref, grad_ref))
        weights = jnp.where(row >= col, jnp.exp(jnp.where(row >= col, since - since_row, 0.0)), 0.0)
        turned = jnp.where(row <= col, jnp.exp(jnp.where(row <= col, since_row - since, 0.0)), 0.0)
        until = jnp.exp(closing - since)
        grad_scores = (matmul_t(g, v) * weights).astype(BF16)
        grad_scores_t = (matmul_t(v, g) * turned).astype(BF16)
        scores_t = (matmul_t(k, q) * turned).astype(BF16)
        dq_ref[:, lanes] = (
            matmul(grad_scores, k) + jnp.exp(since) * matmul_t(g, leading)
        ).astype(BF16)
        dk_ref[:, lanes] = (
            matmul(grad_scores_t, q)
            + until * matmul_t(v, trailing)
        ).astype(BF16)
        dv_ref[:, lanes] = (
            matmul(scores_t, g) + until * matmul(k, trailing)
        ).astype(BF16)


def expert_kernel(capacity, rows_ref, weight_ref, out_ref, total, order):
    step = pl.program_id(0)
    cores, places, sources, lines, _ = rows_ref.shape
    groups = lines // capacity
    tail = capacity - WHOLE
    small = sources * groups * tail
    half = sources * capacity

    @pl.when(step == 0)
    def _():
        row = counting(small)
        f = row // (tail * sources)
        source = (row - f * (tail * sources)) // tail
        slot = row - f * (tail * sources) - source * tail
        order[...] = one_hot(source * (groups * tail) + f * tail + slot, small)

    held = [[rows_ref[c, z] for z in range(places)] for c in range(cores)]
    rest = [one[:, groups * WHOLE :].reshape(small, LANES) for each in held for one in each]
    rest = matmul(order[...], jnp.concatenate(rest, axis=1)).astype(BF16)
    each = small // groups
    left = []
    for c in range(cores):
        whole = [
            held[c][z][:, f * WHOLE : (f + 1) * WHOLE].reshape(sources * WHOLE, LANES)
            for z in range(places)
            for f in range(groups)
        ]
        left.append(jnp.concatenate(whole, axis=1))
        ends = rest[:, c * places * LANES : (c + 1) * places * LANES]
        ends = [
            ends[f * each : (f + 1) * each, z * LANES : (z + 1) * LANES]
            for z in range(places)
            for f in range(groups)
        ]
        left.append(jnp.concatenate(ends, axis=1))
    product = matmul_t(jnp.concatenate(left, axis=0), weight_ref[...])

    @pl.when(step == 0)
    def _():
        total[...] = product

    @pl.when(step > 0)
    def _():
        total[...] += product

    @pl.when(step == pl.num_programs(0) - 1)
    def _():
        lot = WHOLE // tail
        size = cores * lot * capacity
        row = counting(size)
        block = row // capacity
        slot = row - block * capacity
        source = block // cores
        line = jnp.where(slot < WHOLE, source * WHOLE + slot, lot * WHOLE + source * tail + slot - WHOLE)
        place = one_hot(line + (block - source * cores) * (lot * capacity), size)
        for g in range(sources // lot):
            taken = []
            for c in range(cores):
                first = c * half + g * lot * WHOLE
                taken.append(total[first : first + lot * WHOLE])
                first = c * half + sources * WHOLE + g * lot * tail
                taken.append(total[first : first + lot * tail])
            taken = jnp.concatenate(taken, axis=0).astype(BF16)
            out_ref[0, g * size : (g + 1) * size] = matmul(place, taken).astype(BF16)


def per_device(
    queries, keys, values, out_grad, log_decay, moe_grad, expert_ids, gate_weights, down_weight
):
    chips = lax.axis_size("chip")
    blocks = 2 * chips
    experts = chips
    length, width = moe_grad.shape
    decay = log_decay.T
    capacity = 5 * length // (2 * experts)
    heads = log_decay.shape[1]
    lines = width // LANES * capacity
    share = heads * HEAD // blocks
    weight = down_weight[0]
    hidden = weight.shape[0]

    sent = call(
        functools.partial(route_kernel, experts, capacity),
        jax.ShapeDtypeStruct((experts, lines, LANES), BF16),
        2 * experts * lines * 2 * length * width,
        experts * lines * LANES * 2 + length * width * 2,
        name="route",
    )(expert_ids.T, gate_weights.T, moe_grad)
    arrived = lax.all_to_all(sent, "chip", 0, 0, tiled=True)
    gathered = lax.all_gather(arrived, ("core", "exp"), axis=0)

    states = call(
        functools.partial(state_kernel, share),
        jax.ShapeDtypeStruct((blocks, 3 * share, LANES), BF16),
        8 * heads * length * HEAD * HEAD,
        8 * length * width,
        name="states",
    )(queries, keys, values, out_grad, decay)
    states, arrived = lax.optimization_barrier((states, arrived))
    spread = lax.all_to_all(states, ("chip", "core"), 0, 0, tiled=True)
    carried = call(
        functools.partial(scan_kernel, share),
        jax.ShapeDtypeStruct((blocks, 2 * share, LANES), BF16),
        8 * blocks * share * LANES,
        10 * blocks * share * LANES,
        name="scan",
    )(spread)
    carried = lax.all_to_all(carried, ("chip", "core"), 0, 0, tiled=True)
    flat = jax.ShapeDtypeStruct((length, width), BF16)
    query_grad, key_grad, value_grad = call(
        functools.partial(output_kernel, share),
        (flat, flat, flat),
        18 * heads * length * HEAD * HEAD,
        14 * length * width,
        name="outputs",
    )(queries, keys, values, out_grad, decay, carried)

    places = lax.axis_size("exp")
    rows = 2 * chips * capacity
    deep = TOGETHER if places % TOGETHER == 0 else 1
    hidden_grad = call(
        functools.partial(expert_kernel, capacity),
        jax.ShapeDtypeStruct((1, rows, hidden), BF16),
        2 * rows * width * places * hidden,
        2 * (rows + hidden) * width * places,
        grid=(places // deep,),
        in_specs=[
            pl.BlockSpec((2, deep, chips, lines, LANES), lambda z: (0, z, 0, 0, 0)),
            pl.BlockSpec((hidden, deep * width), lambda z: (0, z)),
        ],
        out_specs=pl.BlockSpec((1, rows, hidden), lambda z: (0, 0, 0)),
        scratch_shapes=[
            pltpu.VMEM((rows, hidden), F32),
            pltpu.VMEM(((capacity - WHOLE) * chips * (width // LANES),) * 2, BF16),
        ],
        name="experts",
    )(gathered.reshape(2, places, chips, lines, LANES), weight)
    return (query_grad, key_grad, value_grad, hidden_grad)


def solution(mesh):
    ctx, exp = mesh.devices.shape
    mesh = Mesh(mesh.devices.reshape(ctx // 2, 2, exp), ("chip", "core", "exp"))
    ctx = ("chip", "core")
    in_specs = (
        P(ctx, "exp"),
        P(ctx, "exp"),
        P(ctx, "exp"),
        P(ctx, "exp"),
        P(ctx, "exp"),
        P(ctx, "exp"),
        P(ctx, None),
        P(ctx, None),
        P(ctx, "exp", None),
    )
    out_specs = (P(ctx, "exp"), P(ctx, "exp"), P(ctx, "exp"), P(ctx, None, "exp"))
    return jax.shard_map(
        per_device, mesh=mesh, in_specs=in_specs, out_specs=out_specs, check_vma=False
    )
```

```python
import functools

import jax
import jax.numpy as jnp
from jax import lax
from jax.experimental import pallas as pl
from jax.experimental.pallas import tpu as pltpu
from jax.sharding import Mesh, PartitionSpec as P

F32 = jnp.float32
BF16 = jnp.bfloat16
LANES = 128
HEAD = 128
WHOLE = 8
TOGETHER = 4
INTERPRET = False


def call(kernel, out_shape, flops, moved, **options):
    return pl.pallas_call(
        kernel,
        out_shape=out_shape,
        interpret=INTERPRET,
        cost_estimate=pl.CostEstimate(flops=flops, bytes_accessed=moved, transcendentals=0),
        **options,
    )


def in_hbm(x):
    return x if INTERPRET else pltpu.with_memory_space_constraint(x, pltpu.HBM)


def matmul(a, b):
    return lax.dot_general(a, b, (((1,), (0,)), ((), ())), preferred_element_type=F32)


def matmul_t(a, b):
    return lax.dot_general(a, b, (((1,), (1,)), ((), ())), preferred_element_type=F32)


def pieces(x):
    high = x.astype(BF16)
    rest = x - high.astype(F32)
    middle = rest.astype(BF16)
    return high, middle, (rest - middle.astype(F32)).astype(BF16)


def square(n):
    return (
        lax.broadcasted_iota(jnp.int32, (n, n), 0),
        lax.broadcasted_iota(jnp.int32, (n, n), 1),
    )


def as_column(line, eye):
    return jnp.sum(jnp.where(eye, line, 0.0), axis=1, keepdims=True)


def running_sums(log_decay, row, col):
    upper = jnp.where(row <= col, 1.0, 0.0).astype(BF16)
    high, middle, low = pieces(log_decay)
    return matmul(high, upper) + (matmul(middle, upper) + matmul(low, upper))


def one_hot(want, columns):
    places = lax.broadcasted_iota(jnp.int32, (want.shape[0], columns), 1)
    return jnp.where(places == want, 1.0, 0.0).astype(BF16)


def counting(n):
    return lax.broadcasted_iota(jnp.int32, (n, 1), 0)


def route_kernel(experts, capacity, ids_ref, gate_ref, grad_ref, out_ref):
    length, width = grad_ref.shape
    groups = width // LANES
    tail = capacity - WHOLE
    most = experts * WHOLE
    row, col = square(length)
    eye = row == col
    ids = ids_ref[...].astype(F32)
    grad = grad_ref[...].astype(F32)
    names = [ids[j : j + 1] for j in range(2)]
    numbers = lax.broadcasted_iota(jnp.int32, (experts, length), 0).astype(F32)
    chosen = [jnp.where(numbers == name, 1.0, 0.0) for name in names]
    before = jnp.where(row < col, 1.0, 0.0).astype(BF16)
    counts = matmul((chosen[0] + chosen[1]).astype(BF16), before)
    ranks = [jnp.sum(one * counts, axis=0, keepdims=True) for one in chosen]
    scaled = [(as_column(gate_ref[j : j + 1], eye) * grad).astype(BF16) for j in range(2)]
    codes = [
        jnp.where(rank < WHOLE, name * WHOLE + rank, name * tail + rank + (most - WHOLE))
        for name, rank in zip(names, ranks)
    ]
    code = jnp.concatenate(codes, axis=1).astype(jnp.int32)
    place = lax.broadcasted_iota(jnp.int32, (experts * capacity, 2 * length), 0)
    table = jnp.where(place == code, 1.0, 0.0).astype(BF16)
    routed = matmul(table, jnp.concatenate(scaled, axis=0)).astype(BF16)
    parts = [routed[:, f * LANES : (f + 1) * LANES] for f in range(groups)]
    for f in range(groups):
        out_ref[:, f * WHOLE : (f + 1) * WHOLE] = parts[f][:most].reshape(experts, WHOLE, LANES)
    rest = jnp.concatenate([part[most:] for part in parts], axis=0)
    line = counting(experts * groups * tail)
    expert = line // (groups * tail)
    f = (line - expert * (groups * tail)) // tail
    want = f * (experts * tail) + expert * tail + (line - expert * (groups * tail) - f * tail)
    rest = matmul(one_hot(want, experts * groups * tail), rest).astype(BF16)
    out_ref[:, groups * WHOLE :] = rest.reshape(experts, groups * tail, LANES)


def state_kernel(share, query_ref, key_ref, value_ref, grad_ref, decay_ref, out_ref):
    heads, length = decay_ref.shape
    row, col = square(length)
    running = running_sums(decay_ref[...], row, col)
    per_head = HEAD // share
    lines = lax.broadcasted_iota(jnp.int32, (share, LANES), 0)
    for h in range(heads):
        lanes = slice(h * HEAD, (h + 1) * HEAD)
        since = running[h : h + 1]
        closing = running[h : h + 1, length - 1 : length]
        places = slice(h * per_head, (h + 1) * per_head)
        for at, left, right, factor in (
            (0, key_ref, value_ref, jnp.exp(closing - since)),
            (share, query_ref, grad_ref, jnp.exp(since)),
        ):
            turned = left[:, lanes].astype(F32).T * factor
            high = turned.astype(BF16)
            low = (turned - high.astype(F32)).astype(BF16)
            state = matmul(high, right[:, lanes]) + matmul(low, right[:, lanes])
            out_ref[places, at : at + share] = state.astype(BF16).reshape(per_head, share, LANES)
        high, middle, low = [
            part.astype(F32) for part in pieces(jnp.broadcast_to(jnp.exp(closing), (share, LANES)))
        ]
        decay = jnp.where(lines == 0, high, jnp.where(lines == 1, middle, low))
        out_ref[places, 2 * share : 3 * share] = jnp.broadcast_to(
            decay[None], (per_head, share, LANES)
        ).astype(BF16)


def scan_kernel(share, in_ref, out_ref):
    blocks = in_ref.shape[0]

    def step(carried, b, at):
        held = in_ref[b].astype(F32)
        decay = (held[2 * share : 2 * share + 1] + held[2 * share + 1 : 2 * share + 2]) + held[
            2 * share + 2 : 2 * share + 3
        ]
        return carried, decay * carried + held[at : at + share]

    ahead = jnp.zeros((share, LANES), F32)
    behind = jnp.zeros((share, LANES), F32)
    for b in range(blocks):
        now, ahead = step(ahead, b, 0)
        out_ref[b, 0:share] = now.astype(BF16)
        now, behind = step(behind, blocks - 1 - b, share)
        out_ref[blocks - 1 - b, share : 2 * share] = now.astype(BF16)


def fill_tables(capacity, sources, groups, order_ref, place_ref):
    tail = capacity - WHOLE
    small = sources * groups * tail
    row = counting(small)
    f = row // (tail * sources)
    source = (row - f * (tail * sources)) // tail
    slot = row - f * (tail * sources) - source * tail
    order_ref[...] = one_hot(source * (groups * tail) + f * tail + slot, small)
    lot = WHOLE // tail
    size = 2 * lot * capacity
    row = counting(size)
    block = row // capacity
    slot = row - block * capacity
    source = block // 2
    line = jnp.where(slot < WHOLE, source * WHOLE + slot, lot * WHOLE + source * tail + slot - WHOLE)
    place_ref[...] = one_hot(line + (block - source * 2) * (lot * capacity), size)


def output_kernel(
    share,
    capacity,
    sources,
    query_ref,
    key_ref,
    value_ref,
    grad_ref,
    decay_ref,
    carried_ref,
    dq_ref,
    dk_ref,
    dv_ref,
    order_ref,
    place_ref,
):
    fill_tables(capacity, sources, query_ref.shape[1] // LANES, order_ref, place_ref)
    heads, length = decay_ref.shape
    row, col = square(length)
    eye = row == col
    running = running_sums(decay_ref[...], row, col)
    per_head = HEAD // share
    for h in range(heads):
        lanes = slice(h * HEAD, (h + 1) * HEAD)
        since_row = running[h : h + 1]
        since = as_column(since_row, eye)
        closing = since_row[:, length - 1 : length]
        carried = carried_ref[h * per_head : (h + 1) * per_head]
        leading = carried[:, 0:share].reshape(HEAD, LANES)
        trailing = carried[:, share : 2 * share].reshape(HEAD, LANES)
        q, k, v, g = (ref[:, lanes] for ref in (query_ref, key_ref, value_ref, grad_ref))
        weights = jnp.where(row >= col, jnp.exp(jnp.where(row >= col, since - since_row, 0.0)), 0.0)
        turned = jnp.where(row <= col, jnp.exp(jnp.where(row <= col, since_row - since, 0.0)), 0.0)
        until = jnp.exp(closing - since)
        grad_scores = (matmul_t(g, v) * weights).astype(BF16)
        grad_scores_t = (matmul_t(v, g) * turned).astype(BF16)
        scores_t = (matmul_t(k, q) * turned).astype(BF16)
        dq_ref[:, lanes] = (
            matmul(grad_scores, k) + jnp.exp(since) * matmul_t(g, leading)
        ).astype(BF16)
        dk_ref[:, lanes] = (
            matmul(grad_scores_t, q)
            + until * matmul_t(v, trailing)
        ).astype(BF16)
        dv_ref[:, lanes] = (
            matmul(scores_t, g) + until * matmul(k, trailing)
        ).astype(BF16)


def expert_kernel(capacity, rows_ref, weight_ref, order_ref, place_ref, out_ref, total):
    step = pl.program_id(0)
    cores, places, sources, lines, _ = rows_ref.shape
    groups = lines // capacity
    tail = capacity - WHOLE
    small = sources * groups * tail
    half = sources * capacity

    held = [[rows_ref[c, z] for z in range(places)] for c in range(cores)]
    rest = [one[:, groups * WHOLE :].reshape(small, LANES) for each in held for one in each]
    rest = matmul(order_ref[...], jnp.concatenate(rest, axis=1)).astype(BF16)
    each = small // groups
    left = []
    for c in range(cores):
        whole = [
            held[c][z][:, f * WHOLE : (f + 1) * WHOLE].reshape(sources * WHOLE, LANES)
            for z in range(places)
            for f in range(groups)
        ]
        left.append(jnp.concatenate(whole, axis=1))
        ends = rest[:, c * places * LANES : (c + 1) * places * LANES]
        ends = [
            ends[f * each : (f + 1) * each, z * LANES : (z + 1) * LANES]
            for z in range(places)
            for f in range(groups)
        ]
        left.append(jnp.concatenate(ends, axis=1))
    product = matmul_t(jnp.concatenate(left, axis=0), weight_ref[...])

    @pl.when(step == 0)
    def _():
        total[...] = product

    @pl.when(step > 0)
    def _():
        total[...] += product

    @pl.when(step == pl.num_programs(0) - 1)
    def _():
        lot = WHOLE // tail
        size = cores * lot * capacity
        for g in range(sources // lot):
            taken = []
            for c in range(cores):
                first = c * half + g * lot * WHOLE
                taken.append(total[first : first + lot * WHOLE])
                first = c * half + sources * WHOLE + g * lot * tail
                taken.append(total[first : first + lot * tail])
            taken = jnp.concatenate(taken, axis=0).astype(BF16)
            out_ref[0, g * size : (g + 1) * size] = matmul(place_ref[...], taken).astype(BF16)


def per_device(
    queries, keys, values, out_grad, log_decay, moe_grad, expert_ids, gate_weights, down_weight
):
    chips = lax.axis_size("chip")
    blocks = 2 * chips
    experts = chips
    length, width = moe_grad.shape
    decay = log_decay.T
    capacity = 5 * length // (2 * experts)
    heads = log_decay.shape[1]
    lines = width // LANES * capacity
    share = heads * HEAD // blocks
    weight = down_weight[0]
    hidden = weight.shape[0]

    sent = call(
        functools.partial(route_kernel, experts, capacity),
        jax.ShapeDtypeStruct((experts, lines, LANES), BF16),
        2 * experts * lines * 2 * length * width,
        experts * lines * LANES * 2 + length * width * 2,
        compiler_params=pltpu.CompilerParams(vmem_limit_bytes=16 << 20),
        name="route",
    )(in_hbm(expert_ids.T), in_hbm(gate_weights.T), in_hbm(moe_grad))
    arrived = lax.all_to_all(sent, "chip", 0, 0, tiled=True)
    gathered = lax.all_gather(arrived, ("core", "exp"), axis=0)

    states = call(
        functools.partial(state_kernel, share),
        jax.ShapeDtypeStruct((blocks, 3 * share, LANES), BF16),
        8 * heads * length * HEAD * HEAD,
        8 * length * width,
        name="states",
    )(queries, keys, values, out_grad, decay)
    states, arrived = lax.optimization_barrier((states, arrived))
    spread = lax.all_to_all(states, ("chip", "core"), 0, 0, tiled=True)
    carried = call(
        functools.partial(scan_kernel, share),
        jax.ShapeDtypeStruct((blocks, 2 * share, LANES), BF16),
        8 * blocks * share * LANES,
        10 * blocks * share * LANES,
        name="scan",
    )(spread)
    carried = lax.all_to_all(carried, ("chip", "core"), 0, 0, tiled=True)
    weight, carried = lax.optimization_barrier((weight, carried))
    flat = jax.ShapeDtypeStruct((length, width), BF16)
    small = (capacity - WHOLE) * chips * (width // LANES)
    size = 2 * capacity * (WHOLE // (capacity - WHOLE))
    query_grad, key_grad, value_grad, order, place = call(
        functools.partial(output_kernel, share, capacity, chips),
        (
            flat,
            flat,
            flat,
            jax.ShapeDtypeStruct((small, small), BF16),
            jax.ShapeDtypeStruct((size, size), BF16),
        ),
        18 * heads * length * HEAD * HEAD,
        14 * length * width,
        name="outputs",
    )(queries, keys, values, out_grad, decay, carried)

    places = lax.axis_size("exp")
    rows = 2 * chips * capacity
    deep = TOGETHER if places % TOGETHER == 0 else 1
    hidden_grad = call(
        functools.partial(expert_kernel, capacity),
        jax.ShapeDtypeStruct((1, rows, hidden), BF16),
        2 * rows * width * places * hidden,
        2 * (rows + hidden) * width * places,
        grid=(places // deep,),
        compiler_params=pltpu.CompilerParams(vmem_limit_bytes=24 << 20),
        in_specs=[
            pl.BlockSpec((2, deep, chips, lines, LANES), lambda z: (0, z, 0, 0, 0)),
            pl.BlockSpec((hidden, deep * width), lambda z: (0, z)),
            pl.BlockSpec((small, small), lambda z: (0, 0)),
            pl.BlockSpec((size, size), lambda z: (0, 0)),
        ],
        out_specs=pl.BlockSpec((1, rows, hidden), lambda z: (0, 0, 0)),
        scratch_shapes=[
            pltpu.VMEM((rows, hidden), F32),
        ],
        name="experts",
    )(in_hbm(gathered.reshape(2, places, chips, lines, LANES)), weight, order, place)
    return (query_grad, key_grad, value_grad, hidden_grad)


def solution(mesh):
    ctx, exp = mesh.devices.shape
    mesh = Mesh(mesh.devices.reshape(ctx // 2, 2, exp), ("chip", "core", "exp"))
    ctx = ("chip", "core")
    in_specs = (
        P(ctx, "exp"),
        P(ctx, "exp"),
        P(ctx, "exp"),
        P(ctx, "exp"),
        P(ctx, "exp"),
        P(ctx, "exp"),
        P(ctx, None),
        P(ctx, None),
        P(ctx, "exp", None),
    )
    out_specs = (P(ctx, "exp"), P(ctx, "exp"), P(ctx, "exp"), P(ctx, None, "exp"))
    return jax.shard_map(
        per_device, mesh=mesh, in_specs=in_specs, out_specs=out_specs, check_vma=False
    )
```

```python
import functools

import jax
import jax.numpy as jnp
from jax import lax
from jax.experimental import pallas as pl
from jax.experimental.pallas import tpu as pltpu
from jax.sharding import Mesh, PartitionSpec as P

F32 = jnp.float32
BF16 = jnp.bfloat16
LANES = 128
HEAD = 128
WHOLE = 8
INTERPRET = False


def call(kernel, out_shape, flops, moved, **options):
    return pl.pallas_call(
        kernel,
        out_shape=out_shape,
        interpret=INTERPRET,
        cost_estimate=pl.CostEstimate(flops=flops, bytes_accessed=moved, transcendentals=0),
        **options,
    )


def in_hbm(x):
    return x if INTERPRET else pltpu.with_memory_space_constraint(x, pltpu.HBM)


def matmul(a, b):
    return lax.dot_general(a, b, (((1,), (0,)), ((), ())), preferred_element_type=F32)


def matmul_t(a, b):
    return lax.dot_general(a, b, (((1,), (1,)), ((), ())), preferred_element_type=F32)


def pieces(x):
    high = x.astype(BF16)
    rest = x - high.astype(F32)
    middle = rest.astype(BF16)
    return high, middle, (rest - middle.astype(F32)).astype(BF16)


def square(n):
    return (
        lax.broadcasted_iota(jnp.int32, (n, n), 0),
        lax.broadcasted_iota(jnp.int32, (n, n), 1),
    )


def as_column(line, eye):
    return jnp.sum(jnp.where(eye, line, 0.0), axis=1, keepdims=True)


def running_sums(log_decay, row, col):
    upper = jnp.where(row <= col, 1.0, 0.0).astype(BF16)
    high, middle, low = pieces(log_decay)
    return matmul(high, upper) + (matmul(middle, upper) + matmul(low, upper))


def one_hot(want, columns):
    places = lax.broadcasted_iota(jnp.int32, (want.shape[0], columns), 1)
    return jnp.where(places == want, 1.0, 0.0).astype(BF16)


def counting(n):
    return lax.broadcasted_iota(jnp.int32, (n, 1), 0)


def route_kernel(experts, capacity, ids_ref, gate_ref, grad_ref, out_ref):
    length, width = grad_ref.shape
    groups = width // LANES
    tail = capacity - WHOLE
    most = experts * WHOLE
    row, col = square(length)
    eye = row == col
    ids = ids_ref[...].astype(F32)
    grad = grad_ref[...].astype(F32)
    names = [ids[j : j + 1] for j in range(2)]
    numbers = lax.broadcasted_iota(jnp.int32, (experts, length), 0).astype(F32)
    chosen = [jnp.where(numbers == name, 1.0, 0.0) for name in names]
    before = jnp.where(row < col, 1.0, 0.0).astype(BF16)
    counts = matmul((chosen[0] + chosen[1]).astype(BF16), before)
    ranks = [jnp.sum(one * counts, axis=0, keepdims=True) for one in chosen]
    scaled = [(as_column(gate_ref[j : j + 1], eye) * grad).astype(BF16) for j in range(2)]
    codes = [
        jnp.where(rank < WHOLE, name * WHOLE + rank, name * tail + rank + (most - WHOLE))
        for name, rank in zip(names, ranks)
    ]
    code = jnp.concatenate(codes, axis=1).astype(jnp.int32)
    place = lax.broadcasted_iota(jnp.int32, (experts * capacity, 2 * length), 0)
    table = jnp.where(place == code, 1.0, 0.0).astype(BF16)
    routed = matmul(table, jnp.concatenate(scaled, axis=0)).astype(BF16)
    parts = [routed[:, f * LANES : (f + 1) * LANES] for f in range(groups)]
    for f in range(groups):
        out_ref[:, f * WHOLE : (f + 1) * WHOLE] = parts[f][:most].reshape(experts, WHOLE, LANES)
    rest = jnp.concatenate([part[most:] for part in parts], axis=0)
    line = counting(experts * groups * tail)
    expert = line // (groups * tail)
    f = (line - expert * (groups * tail)) // tail
    want = f * (experts * tail) + expert * tail + (line - expert * (groups * tail) - f * tail)
    rest = matmul(one_hot(want, experts * groups * tail), rest).astype(BF16)
    out_ref[:, groups * WHOLE :] = rest.reshape(experts, groups * tail, LANES)


def state_kernel(share, query_ref, key_ref, value_ref, grad_ref, decay_ref, out_ref):
    heads, length = decay_ref.shape
    row, col = square(length)
    running = running_sums(decay_ref[...], row, col)
    per_head = HEAD // share
    lines = lax.broadcasted_iota(jnp.int32, (share, LANES), 0)
    for h in range(heads):
        lanes = slice(h * HEAD, (h + 1) * HEAD)
        since = running[h : h + 1]
        closing = running[h : h + 1, length - 1 : length]
        places = slice(h * per_head, (h + 1) * per_head)
        for at, left, right, factor in (
            (0, key_ref, value_ref, jnp.exp(closing - since)),
            (share, query_ref, grad_ref, jnp.exp(since)),
        ):
            turned = left[:, lanes].astype(F32).T * factor
            high = turned.astype(BF16)
            low = (turned - high.astype(F32)).astype(BF16)
            state = matmul(high, right[:, lanes]) + matmul(low, right[:, lanes])
            out_ref[places, at : at + share] = state.astype(BF16).reshape(per_head, share, LANES)
        high, middle, low = [
            part.astype(F32) for part in pieces(jnp.broadcast_to(jnp.exp(closing), (share, LANES)))
        ]
        decay = jnp.where(lines == 0, high, jnp.where(lines == 1, middle, low))
        out_ref[places, 2 * share : 3 * share] = jnp.broadcast_to(
            decay[None], (per_head, share, LANES)
        ).astype(BF16)


def scan_kernel(share, in_ref, out_ref):
    blocks = in_ref.shape[0]

    def step(carried, b, at):
        held = in_ref[b].astype(F32)
        decay = (held[2 * share : 2 * share + 1] + held[2 * share + 1 : 2 * share + 2]) + held[
            2 * share + 2 : 2 * share + 3
        ]
        return carried, decay * carried + held[at : at + share]

    ahead = jnp.zeros((share, LANES), F32)
    behind = jnp.zeros((share, LANES), F32)
    for b in range(blocks):
        now, ahead = step(ahead, b, 0)
        out_ref[b, 0:share] = now.astype(BF16)
        now, behind = step(behind, blocks - 1 - b, share)
        out_ref[blocks - 1 - b, share : 2 * share] = now.astype(BF16)


def fill_tables(capacity, sources, groups, order_ref, place_ref):
    tail = capacity - WHOLE
    small = sources * groups * tail
    row = counting(small)
    f = row // (tail * sources)
    source = (row - f * (tail * sources)) // tail
    slot = row - f * (tail * sources) - source * tail
    order_ref[...] = one_hot(source * (groups * tail) + f * tail + slot, small)
    lot = WHOLE // tail
    size = 2 * lot * capacity
    row = counting(size)
    block = row // capacity
    slot = row - block * capacity
    source = block // 2
    line = jnp.where(slot < WHOLE, source * WHOLE + slot, lot * WHOLE + source * tail + slot - WHOLE)
    place_ref[...] = one_hot(line + (block - source * 2) * (lot * capacity), size)


def output_kernel(
    share,
    capacity,
    sources,
    query_ref,
    key_ref,
    value_ref,
    grad_ref,
    decay_ref,
    carried_ref,
    dq_ref,
    dk_ref,
    dv_ref,
    order_ref,
    place_ref,
):
    fill_tables(capacity, sources, query_ref.shape[1] // LANES, order_ref, place_ref)
    heads, length = decay_ref.shape
    row, col = square(length)
    eye = row == col
    running = running_sums(decay_ref[...], row, col)
    per_head = HEAD // share
    for h in range(heads):
        lanes = slice(h * HEAD, (h + 1) * HEAD)
        since_row = running[h : h + 1]
        since = as_column(since_row, eye)
        closing = since_row[:, length - 1 : length]
        carried = carried_ref[h * per_head : (h + 1) * per_head]
        leading = carried[:, 0:share].reshape(HEAD, LANES)
        trailing = carried[:, share : 2 * share].reshape(HEAD, LANES)
        q, k, v, g = (ref[:, lanes] for ref in (query_ref, key_ref, value_ref, grad_ref))
        weights = jnp.where(row >= col, jnp.exp(jnp.where(row >= col, since - since_row, 0.0)), 0.0)
        turned = jnp.where(row <= col, jnp.exp(jnp.where(row <= col, since_row - since, 0.0)), 0.0)
        until = jnp.exp(closing - since)
        grad_scores = (matmul_t(g, v) * weights).astype(BF16)
        grad_scores_t = (matmul_t(v, g) * turned).astype(BF16)
        scores_t = (matmul_t(k, q) * turned).astype(BF16)
        dq_ref[:, lanes] = (
            matmul(grad_scores, k) + jnp.exp(since) * matmul_t(g, leading)
        ).astype(BF16)
        dk_ref[:, lanes] = (
            matmul(grad_scores_t, q)
            + until * matmul_t(v, trailing)
        ).astype(BF16)
        dv_ref[:, lanes] = (
            matmul(scores_t, g) + until * matmul(k, trailing)
        ).astype(BF16)


def expert_kernel(
    capacity,
    turns,
    rows_hbm,
    weight_ref,
    order_hbm,
    place_hbm,
    out_ref,
    rows_ref,
    order_ref,
    place_ref,
    total,
    arrived,
    ready,
):
    cores, _, sources, lines, _ = rows_ref.shape
    groups = lines // capacity
    width = groups * LANES
    tail = capacity - WHOLE
    small = sources * groups * tail
    half = sources * capacity
    tables = [
        pltpu.make_async_copy(order_hbm, order_ref, ready.at[0]),
        pltpu.make_async_copy(place_hbm, place_ref, ready.at[1]),
    ]
    copies = [
        pltpu.make_async_copy(
            rows_hbm.at[:, first:last], rows_ref.at[:, first:last], arrived.at[i]
        )
        for i, (first, last) in enumerate(turns)
    ]
    tables[0].start()
    for copy in copies:
        copy.start()
    tables[1].start()
    tables[0].wait()
    for i, (first, last) in enumerate(turns):
        copies[i].wait()
        count = last - first
        held = [[rows_ref[c, z] for z in range(first, last)] for c in range(cores)]
        rest = [one[:, groups * WHOLE :].reshape(small, LANES) for each in held for one in each]
        rest = matmul(order_ref[...], jnp.concatenate(rest, axis=1)).astype(BF16)
        each = small // groups
        left = []
        for c in range(cores):
            whole = [
                held[c][z][:, f * WHOLE : (f + 1) * WHOLE].reshape(sources * WHOLE, LANES)
                for z in range(count)
                for f in range(groups)
            ]
            left.append(jnp.concatenate(whole, axis=1))
            ends = rest[:, c * count * LANES : (c + 1) * count * LANES]
            ends = [
                ends[f * each : (f + 1) * each, z * LANES : (z + 1) * LANES]
                for z in range(count)
                for f in range(groups)
            ]
            left.append(jnp.concatenate(ends, axis=1))
        product = matmul_t(
            jnp.concatenate(left, axis=0), weight_ref[:, first * width : last * width]
        )
        if i == 0:
            total[...] = product
        else:
            total[...] += product
    tables[1].wait()
    lot = WHOLE // tail
    size = cores * lot * capacity
    for g in range(sources // lot):
        taken = []
        for c in range(cores):
            first = c * half + g * lot * WHOLE
            taken.append(total[first : first + lot * WHOLE])
            first = c * half + sources * WHOLE + g * lot * tail
            taken.append(total[first : first + lot * tail])
        taken = jnp.concatenate(taken, axis=0).astype(BF16)
        out_ref[0, g * size : (g + 1) * size] = matmul(place_ref[...], taken).astype(BF16)


def per_device(
    queries, keys, values, out_grad, log_decay, moe_grad, expert_ids, gate_weights, down_weight
):
    chips = lax.axis_size("chip")
    blocks = 2 * chips
    experts = chips
    length, width = moe_grad.shape
    decay = log_decay.T
    capacity = 5 * length // (2 * experts)
    heads = log_decay.shape[1]
    lines = width // LANES * capacity
    share = heads * HEAD // blocks
    weight = down_weight[0]
    hidden = weight.shape[0]

    sent = call(
        functools.partial(route_kernel, experts, capacity),
        jax.ShapeDtypeStruct((experts, lines, LANES), BF16),
        2 * experts * lines * 2 * length * width,
        experts * lines * LANES * 2 + length * width * 2,
        compiler_params=pltpu.CompilerParams(vmem_limit_bytes=16 << 20),
        name="route",
    )(in_hbm(expert_ids.T), in_hbm(gate_weights.T), in_hbm(moe_grad))
    arrived = lax.all_to_all(sent, "chip", 0, 0, tiled=True)
    gathered = lax.all_gather(arrived, ("core", "exp"), axis=0)

    states = call(
        functools.partial(state_kernel, share),
        jax.ShapeDtypeStruct((blocks, 3 * share, LANES), BF16),
        8 * heads * length * HEAD * HEAD,
        8 * length * width,
        name="states",
    )(queries, keys, values, out_grad, decay)
    states, arrived = lax.optimization_barrier((states, arrived))
    spread = lax.all_to_all(states, ("chip", "core"), 0, 0, tiled=True)
    carried = call(
        functools.partial(scan_kernel, share),
        jax.ShapeDtypeStruct((blocks, 2 * share, LANES), BF16),
        8 * blocks * share * LANES,
        10 * blocks * share * LANES,
        name="scan",
    )(spread)
    carried = lax.all_to_all(carried, ("chip", "core"), 0, 0, tiled=True)
    weight, carried = lax.optimization_barrier((weight, carried))
    flat = jax.ShapeDtypeStruct((length, width), BF16)
    small = (capacity - WHOLE) * chips * (width // LANES)
    size = 2 * capacity * (WHOLE // (capacity - WHOLE))
    query_grad, key_grad, value_grad, order, place = call(
        functools.partial(output_kernel, share, capacity, chips),
        (
            flat,
            flat,
            flat,
            jax.ShapeDtypeStruct((small, small), BF16),
            jax.ShapeDtypeStruct((size, size), BF16),
        ),
        18 * heads * length * HEAD * HEAD,
        14 * length * width,
        name="outputs",
    )(queries, keys, values, out_grad, decay, carried)

    places = lax.axis_size("exp")
    rows = 2 * chips * capacity
    steps = [places * part // 6 for part in (0, 1, 3, 6)]
    turns = [(first, last) for first, last in zip(steps, steps[1:]) if last > first]
    hidden_grad = call(
        functools.partial(expert_kernel, capacity, turns),
        jax.ShapeDtypeStruct((1, rows, hidden), BF16),
        2 * rows * width * places * hidden,
        2 * (rows + hidden) * width * places,
        compiler_params=pltpu.CompilerParams(vmem_limit_bytes=24 << 20),
        in_specs=[
            pl.BlockSpec(memory_space=pl.ANY),
            pl.BlockSpec(memory_space=pltpu.VMEM),
            pl.BlockSpec(memory_space=pl.ANY),
            pl.BlockSpec(memory_space=pl.ANY),
        ],
        out_specs=pl.BlockSpec(memory_space=pltpu.VMEM),
        scratch_shapes=[
            pltpu.VMEM((2, places, chips, lines, LANES), BF16),
            pltpu.VMEM((small, small), BF16),
            pltpu.VMEM((size, size), BF16),
            pltpu.VMEM((rows, hidden), F32),
            pltpu.SemaphoreType.DMA((len(turns),)),
            pltpu.SemaphoreType.DMA((2,)),
        ],
        name="experts",
    )(
        in_hbm(gathered.reshape(2, places, chips, lines, LANES)),
        weight,
        in_hbm(order),
        in_hbm(place),
    )
    return (query_grad, key_grad, value_grad, hidden_grad)


def solution(mesh):
    ctx, exp = mesh.devices.shape
    mesh = Mesh(mesh.devices.reshape(ctx // 2, 2, exp), ("chip", "core", "exp"))
    ctx = ("chip", "core")
    in_specs = (
        P(ctx, "exp"),
        P(ctx, "exp"),
        P(ctx, "exp"),
        P(ctx, "exp"),
        P(ctx, "exp"),
        P(ctx, "exp"),
        P(ctx, None),
        P(ctx, None),
        P(ctx, "exp", None),
    )
    out_specs = (P(ctx, "exp"), P(ctx, "exp"), P(ctx, "exp"), P(ctx, None, "exp"))
    return jax.shard_map(
        per_device, mesh=mesh, in_specs=in_specs, out_specs=out_specs, check_vma=False
    )
```

```python
import functools

import jax
import jax.numpy as jnp
from jax import lax
from jax.experimental import pallas as pl
from jax.experimental.pallas import tpu as pltpu
from jax.sharding import Mesh, PartitionSpec as P

F32 = jnp.float32
BF16 = jnp.bfloat16
LANES = 128
HEAD = 128
WHOLE = 8
TOGETHER = 4
INTERPRET = False


def call(kernel, out_shape, flops, moved, **options):
    return pl.pallas_call(
        kernel,
        out_shape=out_shape,
        interpret=INTERPRET,
        cost_estimate=pl.CostEstimate(flops=flops, bytes_accessed=moved, transcendentals=0),
        **options,
    )


def in_hbm(x):
    return x if INTERPRET else pltpu.with_memory_space_constraint(x, pltpu.HBM)


def matmul(a, b):
    return lax.dot_general(a, b, (((1,), (0,)), ((), ())), preferred_element_type=F32)


def matmul_t(a, b):
    return lax.dot_general(a, b, (((1,), (1,)), ((), ())), preferred_element_type=F32)


def pieces(x):
    high = x.astype(BF16)
    rest = x - high.astype(F32)
    middle = rest.astype(BF16)
    return high, middle, (rest - middle.astype(F32)).astype(BF16)


def square(n):
    return (
        lax.broadcasted_iota(jnp.int32, (n, n), 0),
        lax.broadcasted_iota(jnp.int32, (n, n), 1),
    )


def as_column(line, eye):
    return jnp.sum(jnp.where(eye, line, 0.0), axis=1, keepdims=True)


def running_sums(log_decay, row, col):
    upper = jnp.where(row <= col, 1.0, 0.0).astype(BF16)
    high, middle, low = pieces(log_decay)
    return matmul(high, upper) + (matmul(middle, upper) + matmul(low, upper))


def one_hot(want, columns):
    places = lax.broadcasted_iota(jnp.int32, (want.shape[0], columns), 1)
    return jnp.where(places == want, 1.0, 0.0).astype(BF16)


def counting(n):
    return lax.broadcasted_iota(jnp.int32, (n, 1), 0)


def route_kernel(experts, capacity, ids_ref, gate_ref, grad_ref, out_ref):
    length, width = grad_ref.shape
    groups = width // LANES
    tail = capacity - WHOLE
    most = experts * WHOLE
    row, col = square(length)
    eye = row == col
    ids = ids_ref[...].astype(F32)
    grad = grad_ref[...].astype(F32)
    names = [ids[j : j + 1] for j in range(2)]
    numbers = lax.broadcasted_iota(jnp.int32, (experts, length), 0).astype(F32)
    chosen = [jnp.where(numbers == name, 1.0, 0.0) for name in names]
    before = jnp.where(row < col, 1.0, 0.0).astype(BF16)
    counts = matmul((chosen[0] + chosen[1]).astype(BF16), before)
    ranks = [jnp.sum(one * counts, axis=0, keepdims=True) for one in chosen]
    scaled = [(as_column(gate_ref[j : j + 1], eye) * grad).astype(BF16) for j in range(2)]
    codes = [
        jnp.where(rank < WHOLE, name * WHOLE + rank, name * tail + rank + (most - WHOLE))
        for name, rank in zip(names, ranks)
    ]
    code = jnp.concatenate(codes, axis=1).astype(jnp.int32)
    place = lax.broadcasted_iota(jnp.int32, (experts * capacity, 2 * length), 0)
    table = jnp.where(place == code, 1.0, 0.0).astype(BF16)
    routed = matmul(table, jnp.concatenate(scaled, axis=0)).astype(BF16)
    parts = [routed[:, f * LANES : (f + 1) * LANES] for f in range(groups)]
    for f in range(groups):
        out_ref[:, f * WHOLE : (f + 1) * WHOLE] = parts[f][:most].reshape(experts, WHOLE, LANES)
    rest = jnp.concatenate([part[most:] for part in parts], axis=0)
    line = counting(experts * groups * tail)
    expert = line // (groups * tail)
    f = (line - expert * (groups * tail)) // tail
    want = f * (experts * tail) + expert * tail + (line - expert * (groups * tail) - f * tail)
    rest = matmul(one_hot(want, experts * groups * tail), rest).astype(BF16)
    out_ref[:, groups * WHOLE :] = rest.reshape(experts, groups * tail, LANES)


def state_kernel(share, query_ref, key_ref, value_ref, grad_ref, decay_ref, out_ref):
    heads, length = decay_ref.shape
    row, col = square(length)
    running = running_sums(decay_ref[...], row, col)
    per_head = HEAD // share
    lines = lax.broadcasted_iota(jnp.int32, (share, LANES), 0)
    for h in range(heads):
        lanes = slice(h * HEAD, (h + 1) * HEAD)
        since = running[h : h + 1]
        closing = running[h : h + 1, length - 1 : length]
        places = slice(h * per_head, (h + 1) * per_head)
        for at, left, right, factor in (
            (0, key_ref, value_ref, jnp.exp(closing - since)),
            (share, query_ref, grad_ref, jnp.exp(since)),
        ):
            turned = left[:, lanes].astype(F32).T * factor
            high = turned.astype(BF16)
            low = (turned - high.astype(F32)).astype(BF16)
            state = matmul(high, right[:, lanes]) + matmul(low, right[:, lanes])
            out_ref[places, at : at + share] = state.astype(BF16).reshape(per_head, share, LANES)
        high, middle, low = [
            part.astype(F32) for part in pieces(jnp.broadcast_to(jnp.exp(closing), (share, LANES)))
        ]
        decay = jnp.where(lines == 0, high, jnp.where(lines == 1, middle, low))
        out_ref[places, 2 * share : 3 * share] = jnp.broadcast_to(
            decay[None], (per_head, share, LANES)
        ).astype(BF16)


def scan_kernel(share, in_ref, out_ref):
    blocks = in_ref.shape[0]

    def step(carried, b, at):
        held = in_ref[b].astype(F32)
        decay = (held[2 * share : 2 * share + 1] + held[2 * share + 1 : 2 * share + 2]) + held[
            2 * share + 2 : 2 * share + 3
        ]
        return carried, decay * carried + held[at : at + share]

    ahead = jnp.zeros((share, LANES), F32)
    behind = jnp.zeros((share, LANES), F32)
    for b in range(blocks):
        now, ahead = step(ahead, b, 0)
        out_ref[b, 0:share] = now
        now, behind = step(behind, blocks - 1 - b, share)
        out_ref[blocks - 1 - b, share : 2 * share] = now


def fill_tables(capacity, sources, groups, order_ref, place_ref):
    tail = capacity - WHOLE
    small = sources * groups * tail
    row = counting(small)
    f = row // (tail * sources)
    source = (row - f * (tail * sources)) // tail
    slot = row - f * (tail * sources) - source * tail
    order_ref[...] = one_hot(source * (groups * tail) + f * tail + slot, small)
    lot = WHOLE // tail
    size = 2 * lot * capacity
    row = counting(size)
    block = row // capacity
    slot = row - block * capacity
    source = block // 2
    line = jnp.where(slot < WHOLE, source * WHOLE + slot, lot * WHOLE + source * tail + slot - WHOLE)
    place_ref[...] = one_hot(line + (block - source * 2) * (lot * capacity), size)


def output_kernel(
    share,
    capacity,
    sources,
    query_ref,
    key_ref,
    value_ref,
    grad_ref,
    decay_ref,
    carried_ref,
    dq_ref,
    dk_ref,
    dv_ref,
    order_ref,
    place_ref,
):
    fill_tables(capacity, sources, query_ref.shape[1] // LANES, order_ref, place_ref)
    heads, length = decay_ref.shape
    row, col = square(length)
    eye = row == col
    running = running_sums(decay_ref[...], row, col)
    per_head = HEAD // share
    for h in range(heads):
        lanes = slice(h * HEAD, (h + 1) * HEAD)
        since_row = running[h : h + 1]
        since = as_column(since_row, eye)
        closing = since_row[:, length - 1 : length]
        carried = carried_ref[h * per_head : (h + 1) * per_head]
        leading = pieces(carried[:, 0:share].reshape(HEAD, LANES))
        trailing = pieces(carried[:, share : 2 * share].reshape(HEAD, LANES))
        q, k, v, g = (ref[:, lanes] for ref in (query_ref, key_ref, value_ref, grad_ref))
        weights = jnp.where(row >= col, jnp.exp(jnp.where(row >= col, since - since_row, 0.0)), 0.0)
        turned = jnp.where(row <= col, jnp.exp(jnp.where(row <= col, since_row - since, 0.0)), 0.0)
        until = jnp.exp(closing - since)
        grad_scores = (matmul_t(g, v) * weights).astype(BF16)
        grad_scores_t = (matmul_t(v, g) * turned).astype(BF16)
        scores_t = (matmul_t(k, q) * turned).astype(BF16)
        dq_ref[:, lanes] = (
            matmul(grad_scores, k) + jnp.exp(since) * (matmul_t(g, leading[0]) + matmul_t(g, leading[1]))
        ).astype(BF16)
        dk_ref[:, lanes] = (
            matmul(grad_scores_t, q)
            + until * (matmul_t(v, trailing[0]) + matmul_t(v, trailing[1]))
        ).astype(BF16)
        dv_ref[:, lanes] = (
            matmul(scores_t, g) + until * (matmul(k, trailing[0]) + matmul(k, trailing[1]))
        ).astype(BF16)


def expert_kernel(capacity, rows_ref, weight_ref, order_ref, place_ref, out_ref, total):
    step = pl.program_id(0)
    cores, places, sources, lines, _ = rows_ref.shape
    groups = lines // capacity
    tail = capacity - WHOLE
    small = sources * groups * tail
    half = sources * capacity

    held = [[rows_ref[c, z] for z in range(places)] for c in range(cores)]
    rest = [one[:, groups * WHOLE :].reshape(small, LANES) for each in held for one in each]
    rest = matmul(order_ref[...], jnp.concatenate(rest, axis=1)).astype(BF16)
    each = small // groups
    left = []
    for c in range(cores):
        whole = [
            held[c][z][:, f * WHOLE : (f + 1) * WHOLE].reshape(sources * WHOLE, LANES)
            for z in range(places)
            for f in range(groups)
        ]
        left.append(jnp.concatenate(whole, axis=1))
        ends = rest[:, c * places * LANES : (c + 1) * places * LANES]
        ends = [
            ends[f * each : (f + 1) * each, z * LANES : (z + 1) * LANES]
            for z in range(places)
            for f in range(groups)
        ]
        left.append(jnp.concatenate(ends, axis=1))
    deep = places * groups * LANES
    weight = weight_ref[:, pl.ds(pl.multiple_of(step * deep, deep), deep)]
    product = matmul_t(jnp.concatenate(left, axis=0), weight)

    @pl.when(step == 0)
    def _():
        total[...] = product

    @pl.when(step > 0)
    def _():
        total[...] += product

    @pl.when(step == pl.num_programs(0) - 1)
    def _():
        lot = WHOLE // tail
        size = cores * lot * capacity
        for g in range(sources // lot):
            taken = []
            for c in range(cores):
                first = c * half + g * lot * WHOLE
                taken.append(total[first : first + lot * WHOLE])
                first = c * half + sources * WHOLE + g * lot * tail
                taken.append(total[first : first + lot * tail])
            taken = jnp.concatenate(taken, axis=0).astype(BF16)
            out_ref[0, g * size : (g + 1) * size] = matmul(place_ref[...], taken).astype(BF16)


def per_device(
    queries, keys, values, out_grad, log_decay, moe_grad, expert_ids, gate_weights, down_weight
):
    chips = lax.axis_size("chip")
    blocks = 2 * chips
    experts = chips
    length, width = moe_grad.shape
    decay = log_decay.T
    capacity = 5 * length // (2 * experts)
    heads = log_decay.shape[1]
    lines = width // LANES * capacity
    share = heads * HEAD // blocks
    weight = down_weight[0]
    hidden = weight.shape[0]

    sent = call(
        functools.partial(route_kernel, experts, capacity),
        jax.ShapeDtypeStruct((experts, lines, LANES), BF16),
        2 * experts * lines * 2 * length * width,
        experts * lines * LANES * 2 + length * width * 2,
        compiler_params=pltpu.CompilerParams(vmem_limit_bytes=16 << 20),
        name="route",
    )(in_hbm(expert_ids.T), in_hbm(gate_weights.T), in_hbm(moe_grad))
    arrived = lax.all_to_all(sent, "chip", 0, 0, tiled=True)
    gathered = lax.all_gather(arrived, ("core", "exp"), axis=0)

    states = call(
        functools.partial(state_kernel, share),
        jax.ShapeDtypeStruct((blocks, 3 * share, LANES), BF16),
        8 * heads * length * HEAD * HEAD,
        8 * length * width,
        name="states",
    )(queries, keys, values, out_grad, decay)
    states, arrived = lax.optimization_barrier((states, arrived))
    spread = lax.all_to_all(states, ("chip", "core"), 0, 0, tiled=True)
    carried = call(
        functools.partial(scan_kernel, share),
        jax.ShapeDtypeStruct((blocks, 2 * share, LANES), F32),
        8 * blocks * share * LANES,
        10 * blocks * share * LANES,
        name="scan",
    )(spread)
    carried = lax.all_to_all(carried, ("chip", "core"), 0, 0, tiled=True)
    weight, carried = lax.optimization_barrier((weight, carried))
    flat = jax.ShapeDtypeStruct((length, width), BF16)
    small = (capacity - WHOLE) * chips * (width // LANES)
    size = 2 * capacity * (WHOLE // (capacity - WHOLE))
    query_grad, key_grad, value_grad, order, place = call(
        functools.partial(output_kernel, share, capacity, chips),
        (
            flat,
            flat,
            flat,
            jax.ShapeDtypeStruct((small, small), BF16),
            jax.ShapeDtypeStruct((size, size), BF16),
        ),
        18 * heads * length * HEAD * HEAD,
        14 * length * width,
        name="outputs",
    )(queries, keys, values, out_grad, decay, carried)

    places = lax.axis_size("exp")
    rows = 2 * chips * capacity
    deep = TOGETHER if places % TOGETHER == 0 else 1
    hidden_grad = call(
        functools.partial(expert_kernel, capacity),
        jax.ShapeDtypeStruct((1, rows, hidden), BF16),
        2 * rows * width * places * hidden,
        2 * (rows + hidden) * width * places,
        grid=(places // deep,),
        compiler_params=pltpu.CompilerParams(vmem_limit_bytes=24 << 20),
        in_specs=[
            pl.BlockSpec((2, deep, chips, lines, LANES), lambda z: (0, z, 0, 0, 0)),
            pl.BlockSpec(memory_space=pltpu.VMEM),
            pl.BlockSpec((small, small), lambda z: (0, 0)),
            pl.BlockSpec((size, size), lambda z: (0, 0)),
        ],
        out_specs=pl.BlockSpec((1, rows, hidden), lambda z: (0, 0, 0)),
        scratch_shapes=[
            pltpu.VMEM((rows, hidden), F32),
        ],
        name="experts",
    )(in_hbm(gathered.reshape(2, places, chips, lines, LANES)), weight, in_hbm(order), in_hbm(place))
    return (query_grad, key_grad, value_grad, hidden_grad)


def solution(mesh):
    ctx, exp = mesh.devices.shape
    mesh = Mesh(mesh.devices.reshape(ctx // 2, 2, exp), ("chip", "core", "exp"))
    ctx = ("chip", "core")
    in_specs = (
        P(ctx, "exp"),
        P(ctx, "exp"),
        P(ctx, "exp"),
        P(ctx, "exp"),
        P(ctx, "exp"),
        P(ctx, "exp"),
        P(ctx, None),
        P(ctx, None),
        P(ctx, "exp", None),
    )
    out_specs = (P(ctx, "exp"), P(ctx, "exp"), P(ctx, "exp"), P(ctx, None, "exp"))
    return jax.shard_map(
        per_device, mesh=mesh, in_specs=in_specs, out_specs=out_specs, check_vma=False
    )
```

```python
import functools

import jax
import jax.numpy as jnp
from jax import lax
from jax.experimental import pallas as pl
from jax.experimental.pallas import tpu as pltpu
from jax.sharding import Mesh, PartitionSpec as P

F32 = jnp.float32
BF16 = jnp.bfloat16
LANES = 128
HEAD = 128
WHOLE = 8
TOGETHER = 6
INTERPRET = False


def call(kernel, out_shape, flops, moved, **options):
    return pl.pallas_call(
        kernel,
        out_shape=out_shape,
        interpret=INTERPRET,
        cost_estimate=pl.CostEstimate(flops=flops, bytes_accessed=moved, transcendentals=0),
        **options,
    )


def in_hbm(x):
    return x if INTERPRET else pltpu.with_memory_space_constraint(x, pltpu.HBM)


def matmul(a, b):
    return lax.dot_general(a, b, (((1,), (0,)), ((), ())), preferred_element_type=F32)


def matmul_t(a, b):
    return lax.dot_general(a, b, (((1,), (1,)), ((), ())), preferred_element_type=F32)


def pieces(x):
    high = x.astype(BF16)
    rest = x - high.astype(F32)
    middle = rest.astype(BF16)
    return high, middle, (rest - middle.astype(F32)).astype(BF16)


def square(n):
    return (
        lax.broadcasted_iota(jnp.int32, (n, n), 0),
        lax.broadcasted_iota(jnp.int32, (n, n), 1),
    )


def as_column(line, eye):
    return jnp.sum(jnp.where(eye, line, 0.0), axis=1, keepdims=True)


def running_sums(log_decay, row, col):
    upper = jnp.where(row <= col, 1.0, 0.0).astype(BF16)
    high, middle, low = pieces(log_decay)
    return matmul(high, upper) + (matmul(middle, upper) + matmul(low, upper))


def one_hot(want, columns):
    places = lax.broadcasted_iota(jnp.int32, (want.shape[0], columns), 1)
    return jnp.where(places == want, 1.0, 0.0).astype(BF16)


def counting(n):
    return lax.broadcasted_iota(jnp.int32, (n, 1), 0)


def route_kernel(experts, capacity, ids_ref, gate_ref, grad_ref, out_ref):
    length, width = grad_ref.shape
    groups = width // LANES
    tail = capacity - WHOLE
    most = experts * WHOLE
    row, col = square(length)
    eye = row == col
    ids = ids_ref[...].astype(F32)
    grad = grad_ref[...].astype(F32)
    names = [ids[j : j + 1] for j in range(2)]
    numbers = lax.broadcasted_iota(jnp.int32, (experts, length), 0).astype(F32)
    chosen = [jnp.where(numbers == name, 1.0, 0.0) for name in names]
    before = jnp.where(row < col, 1.0, 0.0).astype(BF16)
    counts = matmul((chosen[0] + chosen[1]).astype(BF16), before)
    ranks = [jnp.sum(one * counts, axis=0, keepdims=True) for one in chosen]
    scaled = [(as_column(gate_ref[j : j + 1], eye) * grad).astype(BF16) for j in range(2)]
    codes = [
        jnp.where(rank < WHOLE, name * WHOLE + rank, name * tail + rank + (most - WHOLE))
        for name, rank in zip(names, ranks)
    ]
    code = jnp.concatenate(codes, axis=1).astype(jnp.int32)
    place = lax.broadcasted_iota(jnp.int32, (experts * capacity, 2 * length), 0)
    table = jnp.where(place == code, 1.0, 0.0).astype(BF16)
    routed = matmul(table, jnp.concatenate(scaled, axis=0)).astype(BF16)
    parts = [routed[:, f * LANES : (f + 1) * LANES] for f in range(groups)]
    for f in range(groups):
        out_ref[:, f * WHOLE : (f + 1) * WHOLE] = parts[f][:most].reshape(experts, WHOLE, LANES)
    rest = jnp.concatenate([part[most:] for part in parts], axis=0)
    line = counting(experts * groups * tail)
    expert = line // (groups * tail)
    f = (line - expert * (groups * tail)) // tail
    want = f * (experts * tail) + expert * tail + (line - expert * (groups * tail) - f * tail)
    rest = matmul(one_hot(want, experts * groups * tail), rest).astype(BF16)
    out_ref[:, groups * WHOLE :] = rest.reshape(experts, groups * tail, LANES)


def state_kernel(share, query_ref, key_ref, value_ref, grad_ref, decay_ref, out_ref):
    heads, length = decay_ref.shape
    row, col = square(length)
    running = running_sums(decay_ref[...], row, col)
    per_head = HEAD // share
    lines = lax.broadcasted_iota(jnp.int32, (share, LANES), 0)
    for h in range(heads):
        lanes = slice(h * HEAD, (h + 1) * HEAD)
        since = running[h : h + 1]
        closing = running[h : h + 1, length - 1 : length]
        places = slice(h * per_head, (h + 1) * per_head)
        for at, left, right, factor in (
            (0, key_ref, value_ref, jnp.exp(closing - since)),
            (share, query_ref, grad_ref, jnp.exp(since)),
        ):
            turned = left[:, lanes].astype(F32).T * factor
            high = turned.astype(BF16)
            low = (turned - high.astype(F32)).astype(BF16)
            state = matmul(high, right[:, lanes]) + matmul(low, right[:, lanes])
            out_ref[places, at : at + share] = state.astype(BF16).reshape(per_head, share, LANES)
        high, middle, low = [
            part.astype(F32) for part in pieces(jnp.broadcast_to(jnp.exp(closing), (share, LANES)))
        ]
        decay = jnp.where(lines == 0, high, jnp.where(lines == 1, middle, low))
        out_ref[places, 2 * share : 3 * share] = jnp.broadcast_to(
            decay[None], (per_head, share, LANES)
        ).astype(BF16)


def scan_kernel(share, in_ref, out_ref):
    blocks = in_ref.shape[0]

    def step(carried, b, at):
        held = in_ref[b].astype(F32)
        decay = (held[2 * share : 2 * share + 1] + held[2 * share + 1 : 2 * share + 2]) + held[
            2 * share + 2 : 2 * share + 3
        ]
        return carried, decay * carried + held[at : at + share]

    ahead = jnp.zeros((share, LANES), F32)
    behind = jnp.zeros((share, LANES), F32)
    for b in range(blocks):
        now, ahead = step(ahead, b, 0)
        out_ref[b, 0:share] = now
        now, behind = step(behind, blocks - 1 - b, share)
        out_ref[blocks - 1 - b, share : 2 * share] = now


def fill_tables(capacity, sources, groups, order_ref, place_ref):
    tail = capacity - WHOLE
    small = sources * groups * tail
    row = counting(small)
    f = row // (tail * sources)
    source = (row - f * (tail * sources)) // tail
    slot = row - f * (tail * sources) - source * tail
    order_ref[...] = one_hot(source * (groups * tail) + f * tail + slot, small)
    lot = WHOLE // tail
    size = 2 * lot * capacity
    row = counting(size)
    block = row // capacity
    slot = row - block * capacity
    source = block // 2
    line = jnp.where(slot < WHOLE, source * WHOLE + slot, lot * WHOLE + source * tail + slot - WHOLE)
    place_ref[...] = one_hot(line + (block - source * 2) * (lot * capacity), size)


def output_kernel(
    share,
    capacity,
    sources,
    query_ref,
    key_ref,
    value_ref,
    grad_ref,
    decay_ref,
    carried_ref,
    dq_ref,
    dk_ref,
    dv_ref,
    order_ref,
    place_ref,
):
    fill_tables(capacity, sources, query_ref.shape[1] // LANES, order_ref, place_ref)
    heads, length = decay_ref.shape
    row, col = square(length)
    eye = row == col
    running = running_sums(decay_ref[...], row, col)
    per_head = HEAD // share
    for h in range(heads):
        lanes = slice(h * HEAD, (h + 1) * HEAD)
        since_row = running[h : h + 1]
        since = as_column(since_row, eye)
        closing = since_row[:, length - 1 : length]
        carried = carried_ref[h * per_head : (h + 1) * per_head]
        leading = pieces(carried[:, 0:share].reshape(HEAD, LANES))
        trailing = pieces(carried[:, share : 2 * share].reshape(HEAD, LANES))
        q, k, v, g = (ref[:, lanes] for ref in (query_ref, key_ref, value_ref, grad_ref))
        weights = jnp.where(row >= col, jnp.exp(jnp.where(row >= col, since - since_row, 0.0)), 0.0)
        turned = jnp.where(row <= col, jnp.exp(jnp.where(row <= col, since_row - since, 0.0)), 0.0)
        until = jnp.exp(closing - since)
        grad_scores = (matmul_t(g, v) * weights).astype(BF16)
        grad_scores_t = (matmul_t(v, g) * turned).astype(BF16)
        scores_t = (matmul_t(k, q) * turned).astype(BF16)
        dq_ref[:, lanes] = (
            matmul(grad_scores, k) + jnp.exp(since) * (matmul_t(g, leading[0]) + matmul_t(g, leading[1]))
        ).astype(BF16)
        dk_ref[:, lanes] = (
            matmul(grad_scores_t, q)
            + until * (matmul_t(v, trailing[0]) + matmul_t(v, trailing[1]))
        ).astype(BF16)
        dv_ref[:, lanes] = (
            matmul(scores_t, g) + until * (matmul(k, trailing[0]) + matmul(k, trailing[1]))
        ).astype(BF16)


def expert_kernel(capacity, rows_ref, weight_ref, order_ref, place_ref, out_ref, total):
    step = pl.program_id(0)
    cores, places, sources, lines, _ = rows_ref.shape
    groups = lines // capacity
    tail = capacity - WHOLE
    small = sources * groups * tail
    half = sources * capacity

    held = [[rows_ref[c, z] for z in range(places)] for c in range(cores)]
    rest = [one[:, groups * WHOLE :].reshape(small, LANES) for each in held for one in each]
    rest = matmul(order_ref[...], jnp.concatenate(rest, axis=1)).astype(BF16)
    each = small // groups
    left = []
    for c in range(cores):
        whole = [
            held[c][z][:, f * WHOLE : (f + 1) * WHOLE].reshape(sources * WHOLE, LANES)
            for z in range(places)
            for f in range(groups)
        ]
        left.append(jnp.concatenate(whole, axis=1))
        ends = rest[:, c * places * LANES : (c + 1) * places * LANES]
        ends = [
            ends[f * each : (f + 1) * each, z * LANES : (z + 1) * LANES]
            for z in range(places)
            for f in range(groups)
        ]
        left.append(jnp.concatenate(ends, axis=1))
    deep = places * groups * LANES
    weight = weight_ref[:, pl.ds(pl.multiple_of(step * deep, deep), deep)]
    product = matmul_t(jnp.concatenate(left, axis=0), weight)

    @pl.when(step == 0)
    def _():
        total[...] = product

    @pl.when(step > 0)
    def _():
        total[...] += product

    @pl.when(step == pl.num_programs(0) - 1)
    def _():
        lot = WHOLE // tail
        size = cores * lot * capacity
        for g in range(sources // lot):
            taken = []
            for c in range(cores):
                first = c * half + g * lot * WHOLE
                taken.append(total[first : first + lot * WHOLE])
                first = c * half + sources * WHOLE + g * lot * tail
                taken.append(total[first : first + lot * tail])
            taken = jnp.concatenate(taken, axis=0).astype(BF16)
            out_ref[0, g * size : (g + 1) * size] = matmul(place_ref[...], taken).astype(BF16)


def per_device(
    queries, keys, values, out_grad, log_decay, moe_grad, expert_ids, gate_weights, down_weight
):
    chips = lax.axis_size("chip")
    blocks = 2 * chips
    experts = chips
    length, width = moe_grad.shape
    decay = log_decay.T
    capacity = 5 * length // (2 * experts)
    heads = log_decay.shape[1]
    lines = width // LANES * capacity
    share = heads * HEAD // blocks
    weight = down_weight[0]
    hidden = weight.shape[0]

    sent = call(
        functools.partial(route_kernel, experts, capacity),
        jax.ShapeDtypeStruct((experts, lines, LANES), BF16),
        2 * experts * lines * 2 * length * width,
        experts * lines * LANES * 2 + length * width * 2,
        compiler_params=pltpu.CompilerParams(vmem_limit_bytes=16 << 20),
        name="route",
    )(in_hbm(expert_ids.T), in_hbm(gate_weights.T), in_hbm(moe_grad))
    arrived = lax.all_to_all(sent, "chip", 0, 0, tiled=True)
    gathered = lax.all_gather(arrived, ("core", "exp"), axis=0)

    states = call(
        functools.partial(state_kernel, share),
        jax.ShapeDtypeStruct((blocks, 3 * share, LANES), BF16),
        8 * heads * length * HEAD * HEAD,
        8 * length * width,
        name="states",
    )(queries, keys, values, out_grad, decay)
    states, arrived = lax.optimization_barrier((states, arrived))
    spread = lax.all_to_all(states, ("chip", "core"), 0, 0, tiled=True)
    carried = call(
        functools.partial(scan_kernel, share),
        jax.ShapeDtypeStruct((blocks, 2 * share, LANES), F32),
        8 * blocks * share * LANES,
        10 * blocks * share * LANES,
        name="scan",
    )(spread)
    carried = lax.all_to_all(carried, ("chip", "core"), 0, 0, tiled=True)
    weight, carried = lax.optimization_barrier((weight, carried))
    flat = jax.ShapeDtypeStruct((length, width), BF16)
    small = (capacity - WHOLE) * chips * (width // LANES)
    size = 2 * capacity * (WHOLE // (capacity - WHOLE))
    query_grad, key_grad, value_grad, order, place = call(
        functools.partial(output_kernel, share, capacity, chips),
        (
            flat,
            flat,
            flat,
            jax.ShapeDtypeStruct((small, small), BF16),
            jax.ShapeDtypeStruct((size, size), BF16),
        ),
        18 * heads * length * HEAD * HEAD,
        14 * length * width,
        name="outputs",
    )(queries, keys, values, out_grad, decay, carried)

    places = lax.axis_size("exp")
    rows = 2 * chips * capacity
    deep = TOGETHER if places % TOGETHER == 0 else 1
    hidden_grad = call(
        functools.partial(expert_kernel, capacity),
        jax.ShapeDtypeStruct((1, rows, hidden), BF16),
        2 * rows * width * places * hidden,
        2 * (rows + hidden) * width * places,
        grid=(places // deep,),
        compiler_params=pltpu.CompilerParams(vmem_limit_bytes=24 << 20),
        in_specs=[
            pl.BlockSpec((2, deep, chips, lines, LANES), lambda z: (0, z, 0, 0, 0)),
            pl.BlockSpec(memory_space=pltpu.VMEM),
            pl.BlockSpec((small, small), lambda z: (0, 0)),
            pl.BlockSpec((size, size), lambda z: (0, 0)),
        ],
        out_specs=pl.BlockSpec((1, rows, hidden), lambda z: (0, 0, 0)),
        scratch_shapes=[
            pltpu.VMEM((rows, hidden), F32),
        ],
        name="experts",
    )(in_hbm(gathered.reshape(2, places, chips, lines, LANES)), weight, in_hbm(order), in_hbm(place))
    return (query_grad, key_grad, value_grad, hidden_grad)


def solution(mesh):
    ctx, exp = mesh.devices.shape
    mesh = Mesh(mesh.devices.reshape(ctx // 2, 2, exp), ("chip", "core", "exp"))
    ctx = ("chip", "core")
    in_specs = (
        P(ctx, "exp"),
        P(ctx, "exp"),
        P(ctx, "exp"),
        P(ctx, "exp"),
        P(ctx, "exp"),
        P(ctx, "exp"),
        P(ctx, None),
        P(ctx, None),
        P(ctx, "exp", None),
    )
    out_specs = (P(ctx, "exp"), P(ctx, "exp"), P(ctx, "exp"), P(ctx, None, "exp"))
    return jax.shard_map(
        per_device, mesh=mesh, in_specs=in_specs, out_specs=out_specs, check_vma=False
    )
```
